32 devices in a mesh: pix: 4 (over y, x), tm: 8 (over z, core).
Axes of the slice: x: 2, y: 2, z: 4, core: 2. Of those that a mesh axis runs over, the one named last changes fastest.
Arguments:
- movie: bfloat16 [80, 128, 1024], P('pix', None, 'tm'), may hold values from -6 to 6
- noise_weight: float32 [80, 128], P('pix'), may hold values from 0.25 to 4
- footprints: bfloat16 [80, 4, 128, 512], P('pix')
- block_ids: int32 [80, 4], P('pix'), may hold values from 0 to 31, as said below
- band_width: int32 [1024], replicated, may hold values from 0 to 5, as said below
- precision_blocks: bfloat16 [11, 128, 128], replicated
Outputs:
- traces: bfloat16 [16384, 1024], P('pix', 'tm')
- residual: bfloat16 [80, 128, 1024], P('pix', None, 'tm')
The draws below stay inside these ranges and needn't reach their ends.
Inputs may be any that keep to these rules, and one draw needn't show every extreme that they name: `block_ids`: each tile names 4 different component blocks. `band_width`: some group has the reach 5.
All inputs are finite; a program needn't handle non-finite values.
Results may differ from the reference program's by a relative error of at most 0.015.
Values may be sent and summed in bfloat16 or wider, within the bound.
A program may use at most 128 MiB of HBM per device.

```python
import math
import jax
import jax.numpy as jnp
from jax import lax

K = 16384
CBLK = 512
TILE = 128
SLOTS = 4
GROUP = 16
BMAX = 5
FR = 128
TILES = 80
T_SIZE = 1024
KB = 32
NG = 1024
GROUPS_DEV = 32
N_PIX = 4


def draw_footprints(key, part):
    scale_top = (3.0 * KB / (TILE * TILES * SLOTS)) ** 0.5
    shape_all = (TILES, SLOTS, TILE, CBLK)
    key_value, key_keep = jax.random.split(jax.random.fold_in(key, 17))
    values = jax.random.uniform(key_value, shape_all, jnp.float32, 0.0, 1.0)
    kept = jax.random.bernoulli(key_keep, 0.1, shape_all).astype(jnp.float32)
    return (values * kept * 10.0 ** 0.5 * scale_top).astype(jnp.bfloat16)


def draw_block_ids(key, part):
    tile_keys = jax.random.split(key, TILES)

    def one_tile(tile_key):
        return jax.random.permutation(tile_key, KB)[:SLOTS]
    return jax.vmap(one_tile)(tile_keys).astype(jnp.int32)


def draw_band_width(key, part):
    key_base, key_hot, key_forced = jax.random.split(key, 3)
    base_reach = jax.random.randint(key_base, (NG,), 0, 3)
    hot_ranges = jax.random.randint(key_hot, (NG // GROUPS_DEV,), 0, 4) == 0
    hot_groups = jnp.repeat(hot_ranges, GROUPS_DEV)
    widths = jnp.where(hot_groups, BMAX, base_reach)
    forced = jax.random.randint(key_forced, (), 0, NG)
    return widths.at[forced].set(BMAX).astype(jnp.int32)


def draw_precision_blocks(key, part):
    offset_count = 2 * BMAX + 1
    offsets = jnp.abs(jnp.arange(offset_count) - BMAX).astype(jnp.float32)
    decay_scale = (0.7 ** offsets)[:, None, None]
    random_part = jax.random.normal(key, (offset_count, FR, FR), jnp.float32)
    blocks = decay_scale * random_part / FR ** 0.5
    identity = jnp.eye(FR, dtype=jnp.float32)
    center = (offsets == 0).astype(jnp.float32)[:, None, None]
    return (blocks + center * identity).astype(jnp.bfloat16)


def shard_levels(key, dims, cuts, smallest, largest):
    gain = 1.0
    for axis_at, blocks in cuts:
        steps = jax.random.uniform(jax.random.fold_in(jax.random.fold_in(key, 6), axis_at), (blocks,), jnp.float32, smallest / len(cuts), largest / len(cuts))
        gain = gain * jnp.repeat(jnp.exp(steps), dims[axis_at] // blocks).reshape((-1,) + (1,) * (len(dims) - 1 - axis_at))
    return gain


def gaussian(rng, dims, deviation, reach, cuts=(), held_as=jnp.bfloat16):
    level = shard_levels(rng, dims, cuts, -0.22, 0.18) if cuts else 1.0
    entries = jax.random.normal(rng, dims, jnp.float32) * deviation * level
    return jnp.minimum(jnp.maximum(entries, -reach), reach).astype(held_as)


def setup_inputs(seed: int = 0) -> dict:
    keys = jax.random.split(jax.random.key(seed), 7)
    return {
        "movie": gaussian(keys[0], (TILES, TILE, T_SIZE), 1.0, 6.0, ((0, 4), (2, 8))),
        "noise_weight": jnp.clip(jnp.exp(math.log(4.0) - 2.7725887 * jax.random.uniform(keys[1], (TILES, TILE), jnp.float32) ** shard_levels(keys[1], (TILES, TILE), ((0, 4),), -0.2, 0.2)), 0.25, 4.0),
        "footprints": draw_footprints(jax.random.fold_in(keys[6], 71), 0),
        "block_ids": draw_block_ids(jax.random.fold_in(keys[6], 71), 0),
        "band_width": draw_band_width(jax.random.fold_in(keys[6], 71), 0),
        "precision_blocks": draw_precision_blocks(jax.random.fold_in(keys[6], 71), 0),
    }


def reference(movie, noise_weight, footprints, block_ids, band_width, precision_blocks):
    frames = movie.shape[2]
    weighted = (noise_weight[:, :, None] * movie.astype(jnp.float32)).astype(jnp.bfloat16)

    def project(running, item):
        feet, idents, pixels = item
        contrib = jnp.einsum('spc,pf->scf', feet.astype(jnp.float32), pixels.astype(jnp.float32))
        return running.at[idents].add(contrib), None

    def one_index(total, item):
        feet, idents, pixels = item
        start = jnp.zeros((K // CBLK, CBLK, frames), jnp.float32)
        part_sum, _ = lax.scan(project, start, (feet, idents, pixels))
        rounded = lax.optimization_barrier(part_sum.astype(jnp.bfloat16)).astype(jnp.float32)
        return total + rounded, None

    tiles_all = movie.shape[0]
    per_index = tiles_all // N_PIX
    grouped = (footprints.reshape(N_PIX, per_index, SLOTS, TILE, CBLK),
               block_ids.reshape(N_PIX, per_index, SLOTS),
               weighted.reshape(N_PIX, per_index, TILE, frames))
    initial = jnp.zeros((K // CBLK, CBLK, frames), jnp.float32)
    summed, _ = lax.scan(one_index, initial, grouped)
    projected = summed.reshape(K, frames).astype(jnp.bfloat16)
    nblocks = frames // FR
    blocks = projected.astype(jnp.float32).reshape(K, nblocks, FR)
    padded = jnp.pad(blocks, ((0, 0), (BMAX, BMAX), (0, 0)))
    widths = jnp.repeat(band_width, GROUP)
    filtered = jnp.zeros((K, nblocks, FR), jnp.float32)
    for offset in range(-BMAX, BMAX + 1):
        shifted = padded[:, BMAX + offset:BMAX + offset + nblocks, :]
        term = jnp.einsum('kbf,fh->kbh', shifted, precision_blocks[offset + BMAX].astype(jnp.float32))
        inside = (abs(offset) <= widths).astype(jnp.float32)
        filtered = filtered + inside[:, None, None] * term
    traces = filtered.reshape(K, frames).astype(jnp.bfloat16)
    trace_blocks = traces.reshape(K // CBLK, CBLK, frames)

    def rebuild(item):
        feet, idents, pixels = item
        chosen = trace_blocks[idents].astype(jnp.float32)
        rebuilt = jnp.einsum('spc,scf->pf', feet.astype(jnp.float32), chosen)
        return (pixels.astype(jnp.float32) - rebuilt).astype(jnp.bfloat16)

    residual = lax.map(rebuild, (footprints, block_ids, movie))
    return traces, residual
```

```python
import functools

import jax
import jax.numpy as jnp
from jax import lax
from jax.experimental import pallas as pl
from jax.experimental.pallas import tpu as pltpu
from jax.sharding import PartitionSpec as P

K = 16384
CBLK = 512
GROUP = 16
BMAX = 5
FR = 128
LANE = 128
SIDE = 2
HALVES = 2
MESH = pl.DeviceIdType.MESH
VMEM_LIMIT = 56 * 1024 * 1024


def tile_batch(tiles):
    return 4 if tiles % 4 == 0 else 1


def project_kernel(ids_ref, movie_ref, noise_ref, feet_ref, out_ref, acc_ref):
    tile = pl.program_id(0)

    @pl.when(tile == 0)
    def _():
        acc_ref[...] = jnp.zeros_like(acc_ref)

    batch, slots = feet_ref.shape[:2]
    for member in range(batch):
        at = tile * batch + member
        pixels = movie_ref[member].astype(jnp.float32)
        weighted = (pixels.T * noise_ref[pl.ds(at, 1), :]).astype(jnp.bfloat16)
        products = [
            jnp.dot(weighted, feet_ref[member, slot], preferred_element_type=jnp.float32)
            for slot in range(slots)
        ]
        for slot in range(slots):
            acc_ref[ids_ref[at, slot]] += products[slot]

    @pl.when(tile == pl.num_programs(0) - 1)
    def _():
        def put(b, carry):
            for c in range(out_ref.shape[0]):
                span = slice(c * LANE, (c + 1) * LANE)
                out_ref[c, b] = acc_ref[b, :, span].astype(out_ref.dtype)
            return carry

        lax.fori_loop(0, out_ref.shape[1], put, 0)


def project(movie, noise_weight, footprints, block_ids):
    tiles, slots, pixels, width = footprints.shape
    frames = movie.shape[2]
    blocks = K // CBLK
    batch = tile_batch(tiles)
    shape = (width // LANE, blocks, frames, LANE)
    return pl.pallas_call(
        project_kernel,
        grid_spec=pltpu.PrefetchScalarGridSpec(
            num_scalar_prefetch=1,
            grid=(tiles // batch,),
            in_specs=[
                pl.BlockSpec((batch, pixels, frames), lambda n, ids: (n, 0, 0)),
                pl.BlockSpec((tiles, pixels), lambda n, ids: (0, 0)),
                pl.BlockSpec((batch, slots, pixels, width), lambda n, ids: (n, 0, 0, 0)),
            ],
            out_specs=pl.BlockSpec(shape, lambda n, ids: (0, 0, 0, 0)),
            scratch_shapes=[pltpu.VMEM((blocks, frames, width), jnp.float32)],
        ),
        out_shape=jax.ShapeDtypeStruct(shape, jnp.bfloat16),
        compiler_params=pltpu.CompilerParams(vmem_limit_bytes=VMEM_LIMIT),
        name="project",
    )(block_ids, movie, noise_weight, footprints)


def rebuild_kernel(ids_ref, me_ref, movie_ref, feet_ref, traces_ref, own_ref, out_ref):
    tile = pl.program_id(0)

    @pl.when(tile == 0)
    def _():
        count = own_ref.shape[0]

        def put(b, carry):
            own_ref[b] = traces_ref[me_ref[0] * count + b]
            return carry

        lax.fori_loop(0, count, put, 0)

    batch, slots = feet_ref.shape[:2]
    for member in range(batch):
        at = tile * batch + member
        rebuilt = None
        for slot in range(slots):
            term = jnp.dot(
                feet_ref[member, slot], traces_ref[ids_ref[at, slot]],
                preferred_element_type=jnp.float32,
            )
            rebuilt = term if rebuilt is None else rebuilt + term
        out_ref[member] = (movie_ref[member].astype(jnp.float32) - rebuilt).astype(out_ref.dtype)


def rebuild(movie, footprints, block_ids, traces):
    tiles, slots, pixels, width = footprints.shape
    frames = movie.shape[2]
    blocks = K // CBLK
    n_pix = lax.axis_size("pix")
    batch = tile_batch(tiles)
    own = (blocks // n_pix, width, frames)
    own_traces, residual = pl.pallas_call(
        rebuild_kernel,
        grid_spec=pltpu.PrefetchScalarGridSpec(
            num_scalar_prefetch=2,
            grid=(tiles // batch,),
            in_specs=[
                pl.BlockSpec((batch, pixels, frames), lambda n, ids, me: (n, 0, 0)),
                pl.BlockSpec((batch, slots, pixels, width), lambda n, ids, me: (n, 0, 0, 0)),
                pl.BlockSpec((blocks, width, frames), lambda n, ids, me: (0, 0, 0)),
            ],
            out_specs=[
                pl.BlockSpec(own, lambda n, ids, me: (0, 0, 0)),
                pl.BlockSpec((batch, pixels, frames), lambda n, ids, me: (n, 0, 0)),
            ],
        ),
        out_shape=[
            jax.ShapeDtypeStruct(own, jnp.bfloat16),
            jax.ShapeDtypeStruct(movie.shape, jnp.bfloat16),
        ],
        compiler_params=pltpu.CompilerParams(vmem_limit_bytes=VMEM_LIMIT),
        name="rebuild",
    )(
        block_ids, lax.axis_index("pix").reshape(1),
        movie, footprints, traces.reshape(blocks, width, frames),
    )
    return own_traces.reshape(K // n_pix, frames), residual


def middle_kernel(
    n_pix, n_tm, ids_ref, band_ref, noise_hbm, prec_hbm, movie_hbm, feet_hbm,
    traces_ref, residual_ref,
    far_buf, near_buf, hop_out, hop_in, x_buf, xt_buf, y_buf,
    prec_t, feet_ref, total_ref, part_ref, sums_ref, weighted_ref,
    movie_ref, noise_ref, prec_ref, table_ref, table_smem,
    far_s, far_r, near_s, near_r, hop_s, hop_r,
    g_s, g_r, relay_s, relay_r, a_s, a_r, b_s, b_r,
    feet_sem, movie_sem, small_sem, *gathered,
):
    chunks, tiles, slots = feet_ref.shape[:3]
    blocks = part_ref.shape[1]
    parts_half = n_tm // HALVES
    batch = tile_batch(tiles)
    pieces = tiles // batch
    nothing = tiles * slots
    me_p = lax.axis_index("pix")
    me_t = lax.axis_index("tm")
    me_x = lax.rem(me_p, SIDE)
    along_x = me_p + 1 - 2 * me_x
    along_y = lax.rem(me_p + SIDE, n_pix)
    across = lax.rem(along_x + SIDE, n_pix)
    first = (along_x, along_y)
    second = (along_y, along_x)

    def tm_at(e):
        return lax.rem(me_t + e, n_tm)

    def part_at(owner, h):
        return pl.ds(owner * n_tm + h * parts_half, parts_half)

    barrier = pltpu.get_barrier_semaphore()
    for peer in first:
        pl.semaphore_signal(barrier, inc=1, device_id={"pix": peer}, device_id_type=MESH)
    for e in range(1, n_tm):
        pl.semaphore_signal(
            barrier, inc=1, device_id={"tm": tm_at(e)}, device_id_type=MESH
        )

    def feet_load(c, k):
        rows = pl.ds(k * batch, batch)
        return pltpu.make_async_copy(
            feet_hbm.at[rows, :, :, pl.ds(c * LANE, LANE)], feet_ref.at[c, rows],
            feet_sem.at[c, k],
        )

    def movie_load(k):
        rows = pl.ds(k * batch, batch)
        return pltpu.make_async_copy(movie_hbm.at[rows], movie_ref.at[rows], movie_sem.at[k])

    load_noise = pltpu.make_async_copy(noise_hbm, noise_ref, small_sem.at[0])
    load_prec = pltpu.make_async_copy(prec_hbm, prec_ref, small_sem.at[1])
    move_table = pltpu.make_async_copy(table_ref, table_smem, small_sem.at[2])

    load_noise.start()
    for k in range(pieces):
        movie_load(k).start()
        feet_load(0, k).start()

    lane = lax.broadcasted_iota(jnp.int32, (8, LANE), 1)

    def name_slots(n, row):
        for s in range(slots):
            row = jnp.where(lane == n * slots + s, ids_ref[s, n], row)
        return row

    named = lax.fori_loop(0, tiles, name_slots, jnp.zeros((8, LANE), jnp.int32))

    def link_slots(n, carry):
        prev, last = carry
        for s in range(slots):
            k = n * slots + s
            block = ids_ref[s, n]
            last = jnp.where(lane == block, k, last)
            prev = jnp.where((named == block) & (lane > k), k, prev)
        return prev, last

    start = jnp.full((8, LANE), nothing, jnp.int32)
    prev, last = lax.fori_loop(0, tiles, link_slots, (start, start))
    table_ref[0:8, :] = prev
    table_ref[8:16, :] = last
    move_table.start()
    sums_ref[nothing] = jnp.zeros(sums_ref.shape[1:], sums_ref.dtype)
    load_noise.wait()
    move_table.wait()

    def project_chunk(c):
        def step(k, carry):
            if c == 0:
                movie_load(k).wait()
            feet_load(c, k).wait()
            for member in range(batch):
                n = k * batch + member
                if c == 0:
                    pixels = movie_ref[n].astype(jnp.float32).T
                    weighted = (pixels * noise_ref[pl.ds(n, 1), :]).astype(jnp.bfloat16)
                    weighted_ref[n] = weighted
                else:
                    weighted = weighted_ref[n]
                feet = jnp.concatenate([feet_ref[c, n, s] for s in range(slots)], axis=1)
                products = jnp.dot(weighted, feet, preferred_element_type=jnp.float32)
                for s in range(slots):
                    at = n * slots + s
                    sums_ref[at] = sums_ref[table_smem[0, at]] + products[:, s * LANE:(s + 1) * LANE]
            return carry

        lax.fori_loop(0, pieces, step, 0)

        def put(b, carry):
            part_ref[c, b] = sums_ref[table_smem[8, b]].astype(part_ref.dtype)
            return carry

        lax.fori_loop(0, blocks, put, 0, unroll=4)

    def pix_copy(source, target, send, recv, c, h, peer):
        return pltpu.make_async_remote_copy(
            src_ref=source, dst_ref=target, send_sem=send.at[c, h], recv_sem=recv.at[c, h],
            device_id={"pix": peer}, device_id_type=MESH,
        )

    def far_copy(c, h):
        source = part_ref.at[c, part_at(across, h)]
        return pix_copy(source, far_buf.at[c, h], far_s, far_r, c, h, first[h])

    def near_copy(c, h):
        source = part_ref.at[c, part_at(first[h], h)]
        return pix_copy(source, near_buf.at[c, h], near_s, near_r, c, h, first[h])

    def hop_copy(c, h):
        return pix_copy(hop_out.at[c, h], hop_in.at[c, h], hop_s, hop_r, c, h, second[h])

    def g_copy(c, h):
        rows = gathered[c].at[pl.ds(me_p * n_tm, n_tm)]
        return pix_copy(rows, rows, g_s, g_r, c, h, first[h])

    def relay_copy(c, h):
        rows = gathered[c].at[part_at(first[h], h)]
        return pix_copy(rows, rows, relay_s, relay_r, c, h, second[h])

    def a_copy(c, e):
        peer = tm_at(e)
        return pltpu.make_async_remote_copy(
            src_ref=x_buf.at[c, peer],
            dst_ref=xt_buf.at[c, me_t + BMAX],
            send_sem=a_s.at[c, e - 1],
            recv_sem=a_r.at[c, e - 1],
            device_id={"tm": peer},
            device_id_type=MESH,
        )

    def b_copy(c, e):
        peer = tm_at(e)
        return pltpu.make_async_remote_copy(
            src_ref=y_buf.at[c, peer],
            dst_ref=gathered[c].at[me_p * n_tm + me_t],
            send_sem=b_s.at[c, e - 1],
            recv_sem=b_r.at[c, e - 1],
            device_id={"tm": peer},
            device_id_type=MESH,
        )

    def send_far(c):
        for h in range(HALVES):
            far_copy(c, h).start()

    def send_near(c):
        for h in range(HALVES):
            near_copy(c, h).start()

    def send_hop(c):
        for h in range(HALVES):
            far_copy(c, h).wait_recv()
            for g in range(parts_half):
                total = part_ref[c, second[h] * n_tm + h * parts_half + g].astype(jnp.float32)
                total = total + far_buf[c, h, g].astype(jnp.float32)
                hop_out[c, h, g] = total.astype(hop_out.dtype)
            hop_copy(c, h).start()

    def sum_chunk(c):
        for h in range(HALVES):
            near_copy(c, h).wait_recv()
            hop_copy(c, h).wait_recv()
            for g in range(parts_half):
                part = h * parts_half + g
                total = part_ref[c, me_p * n_tm + part].astype(jnp.float32)
                total = total + near_buf[c, h, g].astype(jnp.float32)
                total = total + hop_in[c, h, g].astype(jnp.float32)
                x_buf[c, part] = total.astype(x_buf.dtype)
        for e in range(1, n_tm):
            a_copy(c, e).start()
        xt_buf[c, me_t + BMAX] = x_buf[c, me_t]

    def ready_filter():
        load_prec.wait()
        for d in range(prec_ref.shape[0]):
            matrix = prec_ref[d].astype(jnp.float32)
            prec_t[:, d * FR:(d + 1) * FR] = matrix.T.astype(prec_t.dtype)
        edge = jnp.zeros((BMAX,) + xt_buf.shape[2:], xt_buf.dtype)
        for c in range(chunks):
            xt_buf[c, pl.ds(0, BMAX)] = edge
            xt_buf[c, pl.ds(BMAX + n_tm, BMAX)] = edge

    def filter_chunk(c):
        groups = LANE // GROUP
        at = ((me_p * n_tm + me_t) * chunks + c) * groups
        column = lax.broadcasted_iota(jnp.int32, (1, LANE), 1)
        reach = jnp.zeros((1, LANE), jnp.int32)
        for g in range(groups):
            reach = jnp.where(column >= g * GROUP, band_ref[at + g], reach)
        keep = [
            jnp.where(reach >= k, 1.0, 0.0).astype(jnp.bfloat16) for k in range(BMAX + 1)
        ]
        for e in range(1, n_tm):
            a_copy(c, e).wait_recv()

        def one_block(i):
            source = jnp.concatenate(
                [xt_buf[c, i + d + BMAX] * keep[abs(d)] for d in range(-BMAX, BMAX + 1)],
                axis=0,
            )
            result = jnp.dot(prec_t[...], source, preferred_element_type=jnp.float32)
            return result.T.astype(jnp.bfloat16)

        def step(e, carry):
            peer = tm_at(e)
            y_buf[c, peer] = one_block(peer)
            return carry

        lax.fori_loop(0, n_tm, step, 0)
        for e in range(1, n_tm):
            b_copy(c, e).start()
        gathered[c][me_p * n_tm + me_t] = y_buf[c, me_t]

    def gather_chunk(c):
        for e in range(1, n_tm):
            b_copy(c, e).wait_recv()
        for h in range(HALVES):
            g_copy(c, h).start()
        for j in range(n_tm):
            traces_ref[j, c * LANE:(c + 1) * LANE, :] = gathered[c][me_p * n_tm + j]

    def relay_chunk(c):
        for h in range(HALVES):
            g_copy(c, h).wait_recv()
            relay_copy(c, h).start()

    def rebuild_chunk(c):
        for h in range(HALVES):
            relay_copy(c, h).wait_recv()

        def one_tile(n):
            feet = jnp.concatenate([feet_ref[c, n, s] for s in range(slots)], axis=1)
            chosen = jnp.concatenate(
                [gathered[c][ids_ref[s, n]] for s in range(slots)], axis=0
            )
            rebuilt = jnp.dot(feet, chosen, preferred_element_type=jnp.float32)
            if c > 0:
                rebuilt = rebuilt + total_ref[n]
            if c < chunks - 1:
                total_ref[n] = rebuilt
            else:
                left = movie_ref[n].astype(jnp.float32) - rebuilt
                residual_ref[n] = left.astype(residual_ref.dtype)

        def step(k, carry):
            for member in range(batch):
                one_tile(k * batch + member)
            return carry

        lax.fori_loop(0, pieces, step, 0)

    project_chunk(0)
    pl.semaphore_wait(barrier, len(first) + n_tm - 1)
    send_far(0)
    send_near(0)
    load_prec.start()
    for c in range(1, chunks):
        for k in range(pieces):
            feet_load(c, k).start()
    project_chunk(1)
    send_far(1)
    send_hop(0)
    send_near(1)
    project_chunk(2)
    send_far(2)
    send_hop(1)
    send_near(2)
    project_chunk(3)
    send_far(3)
    ready_filter()
    sum_chunk(0)
    send_hop(2)
    send_near(3)
    filter_chunk(0)
    sum_chunk(1)
    send_hop(3)
    gather_chunk(0)
    filter_chunk(1)
    sum_chunk(2)
    sum_chunk(3)
    filter_chunk(2)
    gather_chunk(1)
    relay_chunk(0)
    filter_chunk(3)
    gather_chunk(2)
    relay_chunk(1)
    gather_chunk(3)
    rebuild_chunk(0)
    relay_chunk(2)
    rebuild_chunk(1)
    relay_chunk(3)
    rebuild_chunk(2)
    rebuild_chunk(3)

    for c in range(chunks):
        for h in range(HALVES):
            for copy in (far_copy, near_copy, hop_copy, g_copy, relay_copy):
                copy(c, h).wait_send()
        for e in range(1, n_tm):
            a_copy(c, e).wait_send()
            b_copy(c, e).wait_send()


def middle(movie, noise_weight, footprints, block_ids, band_width, precision_blocks):
    tiles, slots, pixels, width = footprints.shape
    frames = movie.shape[2]
    chunks, blocks, lanes = width // LANE, K // CBLK, LANE
    n_pix, n_tm = lax.axis_size("pix"), lax.axis_size("tm")
    pieces = tiles // tile_batch(tiles)
    dma = pltpu.SemaphoreType.DMA
    bf16, f32 = jnp.bfloat16, jnp.float32
    vmem = pl.BlockSpec(memory_space=pltpu.VMEM)
    smem = pl.BlockSpec(memory_space=pltpu.SMEM)
    part = (frames, lanes)
    traces, residual = pl.pallas_call(
        functools.partial(middle_kernel, n_pix, n_tm),
        out_shape=[
            pltpu.VMEM((n_tm, CBLK, frames), bf16),
            pltpu.VMEM(movie.shape, bf16),
        ],
        in_specs=[smem] * 2 + [pl.BlockSpec(memory_space=pl.ANY)] * 4,
        out_specs=[vmem, vmem],
        scratch_shapes=[pltpu.VMEM((chunks, HALVES, n_tm // HALVES) + part, bf16)] * 4 + [
            pltpu.VMEM((chunks, n_tm) + part, bf16),
            pltpu.VMEM((chunks, n_tm + 2 * BMAX) + part, bf16),
            pltpu.VMEM((chunks, n_tm, lanes, frames), bf16),
            pltpu.VMEM((FR, precision_blocks.shape[0] * FR), bf16),
            pltpu.VMEM((chunks, tiles, slots, pixels, lanes), bf16),
            pltpu.VMEM(movie.shape, f32),
            pltpu.VMEM((chunks, blocks) + part, bf16),
            pltpu.VMEM((tiles * slots + 1,) + part, f32),
            pltpu.VMEM((tiles, frames, pixels), bf16),
            pltpu.VMEM(movie.shape, bf16),
            pltpu.VMEM(noise_weight.shape, f32),
            pltpu.VMEM(precision_blocks.shape, bf16),
            pltpu.VMEM((16, LANE), jnp.int32),
            pltpu.SMEM((16, LANE), jnp.int32),
        ] + [dma((chunks, HALVES))] * 10 + [dma((chunks, n_tm - 1))] * 4
        + [dma((chunks, pieces)), dma((pieces,)), dma((3,))]
        + [pltpu.VMEM((blocks, lanes, frames), bf16)] * chunks,
        compiler_params=pltpu.CompilerParams(
            collective_id=0, has_side_effects=True, vmem_limit_bytes=VMEM_LIMIT
        ),
        name="middle",
    )(block_ids.T, band_width, noise_weight, precision_blocks, movie, footprints)
    return traces.reshape(K // n_pix, frames), residual


def middle_plain(partial_value, movie, footprints, block_ids, band_width, precision_blocks):
    frames = movie.shape[2]
    n_pix, n_tm = lax.axis_size("pix"), lax.axis_size("tm")
    summed = lax.psum_scatter(partial_value, "pix", scatter_dimension=1, tiled=True)
    rows = summed.transpose(1, 0, 3, 2).reshape(K // n_pix, frames)
    moved = lax.all_to_all(rows, "tm", split_axis=0, concat_axis=1, tiled=True)
    here = moved.shape[0]
    start = (lax.axis_index("pix") * n_tm + lax.axis_index("tm")) * here
    widths = lax.dynamic_slice_in_dim(jnp.repeat(band_width, GROUP), start, here)
    nblocks = moved.shape[1] // FR
    padded = jnp.pad(moved.reshape(here, nblocks, FR), ((0, 0), (BMAX, BMAX), (0, 0)))
    filtered = jnp.zeros((here, nblocks, FR), jnp.float32)
    for d in range(2 * BMAX + 1):
        term = jnp.einsum(
            "kbf,fh->kbh", padded[:, d:d + nblocks], precision_blocks[d],
            preferred_element_type=jnp.float32,
        )
        filtered = filtered + jnp.where((abs(d - BMAX) <= widths)[:, None, None], term, 0.0)
    local = filtered.reshape(here, nblocks * FR).astype(jnp.bfloat16)
    traces = lax.all_to_all(local, "tm", split_axis=1, concat_axis=0, tiled=True)
    gathered = lax.all_gather(traces, "pix", axis=0, tiled=True)
    return rebuild(movie, footprints, block_ids, gathered)


def shards(movie, noise_weight, footprints, block_ids, band_width, precision_blocks):
    n_pix, n_tm = lax.axis_size("pix"), lax.axis_size("tm")
    tiles, slots, pixels, width = footprints.shape
    fits = movie.shape[2] == FR and n_pix == SIDE * SIDE and n_pix * n_tm == K // CBLK
    fits = fits and pixels == LANE and tiles * slots <= LANE and width == 4 * LANE
    rest = (movie, footprints, block_ids, band_width, precision_blocks)
    if fits:
        return middle(movie, noise_weight, *rest[1:])
    return middle_plain(project(movie, noise_weight, footprints, block_ids), *rest)


def solution(mesh):
    return jax.shard_map(
        shards,
        mesh=mesh,
        in_specs=(
            P("pix", None, "tm"),
            P("pix", None),
            P("pix", None, None, None),
            P("pix", None),
            P(),
            P(),
        ),
        out_specs=(P("pix", "tm"), P("pix", None, "tm")),
        check_vma=False,
    )
```

```python
import functools

import jax
import jax.numpy as jnp
from jax import lax
from jax.experimental import pallas as pl
from jax.experimental.pallas import tpu as pltpu
from jax.sharding import PartitionSpec as P

K = 16384
CBLK = 512
GROUP = 16
BMAX = 5
FR = 128
LANE = 128
SIDE = 2
HALVES = 2
SPLIT_SUM = (2, 2, 2, 1)
SPLIT_TRACE = (1, 2, 2, 2)
MESH = pl.DeviceIdType.MESH
VMEM_LIMIT = 56 * 1024 * 1024


def tile_batch(tiles):
    return 4 if tiles % 4 == 0 else 1


def project_kernel(ids_ref, movie_ref, noise_ref, feet_ref, out_ref, acc_ref):
    tile = pl.program_id(0)

    @pl.when(tile == 0)
    def _():
        acc_ref[...] = jnp.zeros_like(acc_ref)

    batch, slots = feet_ref.shape[:2]
    for member in range(batch):
        at = tile * batch + member
        pixels = movie_ref[member].astype(jnp.float32)
        weighted = (pixels.T * noise_ref[pl.ds(at, 1), :]).astype(jnp.bfloat16)
        products = [
            jnp.dot(weighted, feet_ref[member, slot], preferred_element_type=jnp.float32)
            for slot in range(slots)
        ]
        for slot in range(slots):
            acc_ref[ids_ref[at, slot]] += products[slot]

    @pl.when(tile == pl.num_programs(0) - 1)
    def _():
        def put(b, carry):
            for c in range(out_ref.shape[0]):
                span = slice(c * LANE, (c + 1) * LANE)
                out_ref[c, b] = acc_ref[b, :, span].astype(out_ref.dtype)
            return carry

        lax.fori_loop(0, out_ref.shape[1], put, 0)


def project(movie, noise_weight, footprints, block_ids):
    tiles, slots, pixels, width = footprints.shape
    frames = movie.shape[2]
    blocks = K // CBLK
    batch = tile_batch(tiles)
    shape = (width // LANE, blocks, frames, LANE)
    return pl.pallas_call(
        project_kernel,
        grid_spec=pltpu.PrefetchScalarGridSpec(
            num_scalar_prefetch=1,
            grid=(tiles // batch,),
            in_specs=[
                pl.BlockSpec((batch, pixels, frames), lambda n, ids: (n, 0, 0)),
                pl.BlockSpec((tiles, pixels), lambda n, ids: (0, 0)),
                pl.BlockSpec((batch, slots, pixels, width), lambda n, ids: (n, 0, 0, 0)),
            ],
            out_specs=pl.BlockSpec(shape, lambda n, ids: (0, 0, 0, 0)),
            scratch_shapes=[pltpu.VMEM((blocks, frames, width), jnp.float32)],
        ),
        out_shape=jax.ShapeDtypeStruct(shape, jnp.bfloat16),
        compiler_params=pltpu.CompilerParams(vmem_limit_bytes=VMEM_LIMIT),
        name="project",
    )(block_ids, movie, noise_weight, footprints)


def rebuild_kernel(ids_ref, me_ref, movie_ref, feet_ref, traces_ref, own_ref, out_ref):
    tile = pl.program_id(0)

    @pl.when(tile == 0)
    def _():
        count = own_ref.shape[0]

        def put(b, carry):
            own_ref[b] = traces_ref[me_ref[0] * count + b]
            return carry

        lax.fori_loop(0, count, put, 0)

    batch, slots = feet_ref.shape[:2]
    for member in range(batch):
        at = tile * batch + member
        rebuilt = None
        for slot in range(slots):
            term = jnp.dot(
                feet_ref[member, slot], traces_ref[ids_ref[at, slot]],
                preferred_element_type=jnp.float32,
            )
            rebuilt = term if rebuilt is None else rebuilt + term
        out_ref[member] = (movie_ref[member].astype(jnp.float32) - rebuilt).astype(out_ref.dtype)


def rebuild(movie, footprints, block_ids, traces):
    tiles, slots, pixels, width = footprints.shape
    frames = movie.shape[2]
    blocks = K // CBLK
    n_pix = lax.axis_size("pix")
    batch = tile_batch(tiles)
    own = (blocks // n_pix, width, frames)
    own_traces, residual = pl.pallas_call(
        rebuild_kernel,
        grid_spec=pltpu.PrefetchScalarGridSpec(
            num_scalar_prefetch=2,
            grid=(tiles // batch,),
            in_specs=[
                pl.BlockSpec((batch, pixels, frames), lambda n, ids, me: (n, 0, 0)),
                pl.BlockSpec((batch, slots, pixels, width), lambda n, ids, me: (n, 0, 0, 0)),
                pl.BlockSpec((blocks, width, frames), lambda n, ids, me: (0, 0, 0)),
            ],
            out_specs=[
                pl.BlockSpec(own, lambda n, ids, me: (0, 0, 0)),
                pl.BlockSpec((batch, pixels, frames), lambda n, ids, me: (n, 0, 0)),
            ],
        ),
        out_shape=[
            jax.ShapeDtypeStruct(own, jnp.bfloat16),
            jax.ShapeDtypeStruct(movie.shape, jnp.bfloat16),
        ],
        compiler_params=pltpu.CompilerParams(vmem_limit_bytes=VMEM_LIMIT),
        name="rebuild",
    )(
        block_ids, lax.axis_index("pix").reshape(1),
        movie, footprints, traces.reshape(blocks, width, frames),
    )
    return own_traces.reshape(K // n_pix, frames), residual


def middle_kernel(
    n_pix, n_tm, ids_ref, band_ref, noise_hbm, prec_hbm, movie_hbm, feet_hbm,
    traces_ref, residual_ref,
    far_buf, near_buf, hop_out, hop_in, x_buf, xt_buf, y_buf,
    prec_t, feet_ref, total_ref, part_ref, sums_ref, weighted_ref,
    movie_ref, noise_ref, prec_ref, table_ref, table_smem,
    far_s, far_r, near_s, near_r, hop_s, hop_r,
    g_s, g_r, relay_s, relay_r, a_s, a_r, b_s, b_r,
    feet_sem, movie_sem, small_sem, *gathered,
):
    chunks, tiles, slots = feet_ref.shape[:3]
    blocks = part_ref.shape[1]
    parts_half = n_tm // HALVES
    batch = tile_batch(tiles)
    pieces = tiles // batch
    nothing = tiles * slots
    me_p = lax.axis_index("pix")
    me_t = lax.axis_index("tm")
    me_x = lax.rem(me_p, SIDE)
    along_x = me_p + 1 - 2 * me_x
    along_y = lax.rem(me_p + SIDE, n_pix)
    across = lax.rem(along_x + SIDE, n_pix)
    first = (along_x, along_y)
    second = (along_y, along_x)

    far_first = sorted(range(1, n_tm), key=lambda e: abs(2 * e - n_tm))

    def tm_at(e):
        return lax.rem(me_t + e, n_tm)

    def part_at(owner, h):
        return pl.ds(owner * n_tm + h * parts_half, parts_half)

    barrier = pltpu.get_barrier_semaphore()
    for peer in first:
        pl.semaphore_signal(barrier, inc=1, device_id={"pix": peer}, device_id_type=MESH)
    for e in range(1, n_tm):
        pl.semaphore_signal(
            barrier, inc=1, device_id={"tm": tm_at(e)}, device_id_type=MESH
        )

    def feet_load(c, k):
        rows = pl.ds(k * batch, batch)
        return pltpu.make_async_copy(
            feet_hbm.at[rows, :, :, pl.ds(c * LANE, LANE)], feet_ref.at[c, rows],
            feet_sem.at[c, k],
        )

    def movie_load(k):
        rows = pl.ds(k * batch, batch)
        return pltpu.make_async_copy(movie_hbm.at[rows], movie_ref.at[rows], movie_sem.at[k])

    load_noise = pltpu.make_async_copy(noise_hbm, noise_ref, small_sem.at[0])
    load_prec = pltpu.make_async_copy(prec_hbm, prec_ref, small_sem.at[1])
    move_table = pltpu.make_async_copy(table_ref, table_smem, small_sem.at[2])

    load_noise.start()
    for k in range(pieces):
        movie_load(k).start()
        feet_load(0, k).start()

    lane = lax.broadcasted_iota(jnp.int32, (8, LANE), 1)

    def name_slots(n, row):
        for s in range(slots):
            row = jnp.where(lane == n * slots + s, ids_ref[s, n], row)
        return row

    named = lax.fori_loop(0, tiles, name_slots, jnp.zeros((8, LANE), jnp.int32))

    def link_slots(n, carry):
        prev, last = carry
        for s in range(slots):
            k = n * slots + s
            block = ids_ref[s, n]
            last = jnp.where(lane == block, k, last)
            prev = jnp.where((named == block) & (lane > k), k, prev)
        return prev, last

    start = jnp.full((8, LANE), nothing, jnp.int32)
    prev, last = lax.fori_loop(0, tiles, link_slots, (start, start))
    table_ref[0:8, :] = prev
    table_ref[8:16, :] = last
    move_table.start()
    sums_ref[nothing] = jnp.zeros(sums_ref.shape[1:], sums_ref.dtype)
    load_noise.wait()
    move_table.wait()

    def project_chunk(c):
        def step(k, carry):
            if c == 0:
                movie_load(k).wait()
            feet_load(c, k).wait()
            for member in range(batch):
                n = k * batch + member
                if c == 0:
                    pixels = movie_ref[n].astype(jnp.float32).T
                    weighted = (pixels * noise_ref[pl.ds(n, 1), :]).astype(jnp.bfloat16)
                    weighted_ref[n] = weighted
                else:
                    weighted = weighted_ref[n]
                feet = jnp.concatenate([feet_ref[c, n, s] for s in range(slots)], axis=1)
                products = jnp.dot(weighted, feet, preferred_element_type=jnp.float32)
                for s in range(slots):
                    at = n * slots + s
                    sums_ref[at] = sums_ref[table_smem[0, at]] + products[:, s * LANE:(s + 1) * LANE]
            return carry

        lax.fori_loop(0, pieces, step, 0)

        def put(b, carry):
            part_ref[c, b] = sums_ref[table_smem[8, b]].astype(part_ref.dtype)
            return carry

        lax.fori_loop(0, blocks, put, 0, unroll=4)

    def rows_at(split, c, u):
        size = FR // split[c]
        return pl.ds(u * size, size)

    def pix_copy(source, target, send, recv, at, peer):
        return pltpu.make_async_remote_copy(
            src_ref=source, dst_ref=target, send_sem=send.at[at], recv_sem=recv.at[at],
            device_id={"pix": peer}, device_id_type=MESH,
        )

    def tm_copy(source, target, send, recv, at, peer):
        return pltpu.make_async_remote_copy(
            src_ref=source, dst_ref=target, send_sem=send.at[at], recv_sem=recv.at[at],
            device_id={"tm": peer}, device_id_type=MESH,
        )

    def far_copy(c, u, h):
        rows = rows_at(SPLIT_SUM, c, u)
        source = part_ref.at[c, part_at(across, h), rows]
        return pix_copy(source, far_buf.at[c, h, :, rows], far_s, far_r, (c, u, h), first[h])

    def near_copy(c, u, h):
        rows = rows_at(SPLIT_SUM, c, u)
        source = part_ref.at[c, part_at(first[h], h), rows]
        return pix_copy(source, near_buf.at[c, h, :, rows], near_s, near_r, (c, u, h), first[h])

    def hop_copy(c, u, h):
        rows = rows_at(SPLIT_SUM, c, u)
        return pix_copy(
            hop_out.at[c, h, :, rows], hop_in.at[c, h, :, rows], hop_s, hop_r, (c, u, h), second[h]
        )

    def g_copy(c, u, h):
        part = gathered[c].at[pl.ds(me_p * n_tm, n_tm), rows_at(SPLIT_TRACE, c, u)]
        return pix_copy(part, part, g_s, g_r, (c, u, h), first[h])

    def relay_copy(c, u, h):
        part = gathered[c].at[part_at(first[h], h), rows_at(SPLIT_TRACE, c, u)]
        return pix_copy(part, part, relay_s, relay_r, (c, u, h), second[h])

    def a_copy(c, u, e):
        rows = rows_at(SPLIT_SUM, c, u)
        peer = tm_at(e)
        source = x_buf.at[c, peer, rows]
        return tm_copy(source, xt_buf.at[c, me_t, rows], a_s, a_r, (c, u, e - 1), peer)

    def b_copy(c, u, e):
        rows = rows_at(SPLIT_TRACE, c, u)
        peer = tm_at(e)
        target = gathered[c].at[me_p * n_tm + me_t, rows]
        return tm_copy(y_buf.at[c, peer, rows], target, b_s, b_r, (c, u, e - 1), peer)

    def send_far(c, u=0):
        for h in range(HALVES):
            far_copy(c, u, h).start()

    def send_near(c, u=0):
        for h in range(HALVES):
            near_copy(c, u, h).start()

    def send_hop(c, u=0):
        rows = rows_at(SPLIT_SUM, c, u)
        for h in range(HALVES):
            far_copy(c, u, h).wait_recv()
            for g in range(parts_half):
                own = part_ref[c, second[h] * n_tm + h * parts_half + g, rows]
                total = own.astype(jnp.float32) + far_buf[c, h, g, rows].astype(jnp.float32)
                hop_out[c, h, g, rows] = total.astype(hop_out.dtype)
            hop_copy(c, u, h).start()

    def sum_chunk(c, u=0):
        rows = rows_at(SPLIT_SUM, c, u)
        for h in range(HALVES):
            near_copy(c, u, h).wait_recv()
            hop_copy(c, u, h).wait_recv()
            for g in range(parts_half):
                part = h * parts_half + g
                total = part_ref[c, me_p * n_tm + part, rows].astype(jnp.float32)
                total = total + near_buf[c, h, g, rows].astype(jnp.float32)
                total = total + hop_in[c, h, g, rows].astype(jnp.float32)
                x_buf[c, part, rows] = total.astype(x_buf.dtype)
        for e in far_first:
            a_copy(c, u, e).start()
        xt_buf[c, me_t, rows] = x_buf[c, me_t, rows]

    def ready_filter():
        load_prec.wait()
        for d in range(prec_ref.shape[0]):
            matrix = prec_ref[d].astype(jnp.float32)
            prec_t[:, d * FR:(d + 1) * FR] = matrix.T.astype(prec_t.dtype)

    def filter_chunk(c):
        groups = LANE // GROUP
        at = ((me_p * n_tm + me_t) * chunks + c) * groups
        column = lax.broadcasted_iota(jnp.int32, (1, LANE), 1)
        reach = jnp.zeros((1, LANE), jnp.int32)
        for g in range(groups):
            reach = jnp.where(column >= g * GROUP, band_ref[at + g], reach)
        keep = [
            jnp.where(reach >= k, 1.0, 0.0).astype(jnp.bfloat16) for k in range(BMAX + 1)
        ]
        for u in range(SPLIT_SUM[c]):
            for e in far_first:
                a_copy(c, u, e).wait_recv()

        for i in range(n_tm):
            low, high = max(0, i - BMAX), min(n_tm, i + BMAX + 1)
            source = jnp.concatenate(
                [xt_buf[c, j] * keep[abs(j - i)] for j in range(low, high)], axis=0
            )
            bands = prec_t[:, (low - i + BMAX) * FR:(high - i + BMAX) * FR]
            result = jnp.dot(bands, source, preferred_element_type=jnp.float32)
            y_buf[c, i] = result.T.astype(jnp.bfloat16)

        for u in range(SPLIT_TRACE[c]):
            for e in far_first:
                b_copy(c, u, e).start()
        gathered[c][me_p * n_tm + me_t] = y_buf[c, me_t]

    def gather_chunk(c, u=0):
        for e in far_first:
            b_copy(c, u, e).wait_recv()
        for h in range(HALVES):
            g_copy(c, u, h).start()
        size = FR // SPLIT_TRACE[c]
        span = slice(c * LANE + u * size, c * LANE + (u + 1) * size)
        for j in range(n_tm):
            traces_ref[j, span, :] = gathered[c][me_p * n_tm + j, rows_at(SPLIT_TRACE, c, u)]

    def relay_chunk(c, u=0):
        for h in range(HALVES):
            g_copy(c, u, h).wait_recv()
            relay_copy(c, u, h).start()

    def rebuild_chunk(c):
        for u in range(SPLIT_TRACE[c]):
            for h in range(HALVES):
                relay_copy(c, u, h).wait_recv()

        def one_tile(n):
            feet = jnp.concatenate([feet_ref[c, n, s] for s in range(slots)], axis=1)
            chosen = jnp.concatenate(
                [gathered[c][ids_ref[s, n]] for s in range(slots)], axis=0
            )
            rebuilt = jnp.dot(feet, chosen, preferred_element_type=jnp.float32)
            if c > 0:
                rebuilt = rebuilt + total_ref[n]
            if c < chunks - 1:
                total_ref[n] = rebuilt
            else:
                left = movie_ref[n].astype(jnp.float32) - rebuilt
                residual_ref[n] = left.astype(residual_ref.dtype)

        def step(k, carry):
            for member in range(batch):
                one_tile(k * batch + member)
            return carry

        lax.fori_loop(0, pieces, step, 0)

    project_chunk(0)
    pl.semaphore_wait(barrier, len(first) + n_tm - 1)
    send_far(0, 0)
    send_near(0, 0)
    send_far(0, 1)
    load_prec.start()
    for c in range(1, chunks):
        for k in range(pieces):
            feet_load(c, k).start()
    project_chunk(1)
    ready_filter()
    send_hop(0, 0)
    send_near(0, 1)
    send_far(1, 0)
    project_chunk(2)
    send_hop(0, 1)
    sum_chunk(0, 0)
    send_near(1, 0)
    send_hop(1, 0)
    sum_chunk(0, 1)
    send_far(1, 1)
    send_near(1, 1)
    project_chunk(3)
    send_far(2, 0)
    sum_chunk(1, 0)
    send_hop(1, 1)
    send_far(2, 1)
    send_near(2, 0)
    filter_chunk(0)
    send_hop(2, 0)
    send_far(3, 0)
    send_hop(2, 1)
    sum_chunk(1, 1)
    send_near(2, 1)
    send_hop(3, 0)
    sum_chunk(2, 0)
    send_near(3, 0)
    filter_chunk(1)
    gather_chunk(0, 0)
    gather_chunk(1, 0)
    sum_chunk(2, 1)
    sum_chunk(3, 0)
    gather_chunk(1, 1)
    relay_chunk(0, 0)
    filter_chunk(2)
    relay_chunk(1, 0)
    relay_chunk(1, 1)
    gather_chunk(2, 0)
    filter_chunk(3)
    gather_chunk(2, 1)
    relay_chunk(2, 0)
    gather_chunk(3, 0)
    rebuild_chunk(0)
    gather_chunk(3, 1)
    relay_chunk(2, 1)
    rebuild_chunk(1)
    relay_chunk(3, 0)
    relay_chunk(3, 1)
    rebuild_chunk(2)
    rebuild_chunk(3)
    for c in range(chunks):
        for u in range(SPLIT_SUM[c]):
            for h in range(HALVES):
                for copy in (far_copy, near_copy, hop_copy):
                    copy(c, u, h).wait_send()
            for e in far_first:
                a_copy(c, u, e).wait_send()
        for u in range(SPLIT_TRACE[c]):
            for h in range(HALVES):
                for copy in (g_copy, relay_copy):
                    copy(c, u, h).wait_send()
            for e in far_first:
                b_copy(c, u, e).wait_send()


def middle(movie, noise_weight, footprints, block_ids, band_width, precision_blocks):
    tiles, slots, pixels, width = footprints.shape
    frames = movie.shape[2]
    chunks, blocks, lanes = width // LANE, K // CBLK, LANE
    n_pix, n_tm = lax.axis_size("pix"), lax.axis_size("tm")
    pieces = tiles // tile_batch(tiles)
    dma = pltpu.SemaphoreType.DMA
    bf16, f32 = jnp.bfloat16, jnp.float32
    vmem = pl.BlockSpec(memory_space=pltpu.VMEM)
    smem = pl.BlockSpec(memory_space=pltpu.SMEM)
    part = (frames, lanes)
    traces, residual = pl.pallas_call(
        functools.partial(middle_kernel, n_pix, n_tm),
        out_shape=[
            pltpu.VMEM((n_tm, CBLK, frames), bf16),
            pltpu.VMEM(movie.shape, bf16),
        ],
        in_specs=[smem] * 2 + [pl.BlockSpec(memory_space=pl.ANY)] * 4,
        out_specs=[vmem, vmem],
        scratch_shapes=[pltpu.VMEM((chunks, HALVES, n_tm // HALVES) + part, bf16)] * 4 + [
            pltpu.VMEM((chunks, n_tm) + part, bf16),
            pltpu.VMEM((chunks, n_tm) + part, bf16),
            pltpu.VMEM((chunks, n_tm, lanes, frames), bf16),
            pltpu.VMEM((FR, precision_blocks.shape[0] * FR), bf16),
            pltpu.VMEM((chunks, tiles, slots, pixels, lanes), bf16),
            pltpu.VMEM(movie.shape, f32),
            pltpu.VMEM((chunks, blocks) + part, bf16),
            pltpu.VMEM((tiles * slots + 1,) + part, f32),
            pltpu.VMEM((tiles, frames, pixels), bf16),
            pltpu.VMEM(movie.shape, bf16),
            pltpu.VMEM(noise_weight.shape, f32),
            pltpu.VMEM(precision_blocks.shape, bf16),
            pltpu.VMEM((16, LANE), jnp.int32),
            pltpu.SMEM((16, LANE), jnp.int32),
        ] + [dma((chunks, 2, HALVES))] * 10 + [dma((chunks, 2, n_tm - 1))] * 4
        + [dma((chunks, pieces)), dma((pieces,)), dma((3,))]
        + [pltpu.VMEM((blocks, lanes, frames), bf16)] * chunks,
        compiler_params=pltpu.CompilerParams(
            collective_id=0, has_side_effects=True, vmem_limit_bytes=VMEM_LIMIT
        ),
        name="middle",
    )(block_ids.T, band_width, noise_weight, precision_blocks, movie, footprints)
    return traces.reshape(K // n_pix, frames), residual


def middle_plain(partial_value, movie, footprints, block_ids, band_width, precision_blocks):
    frames = movie.shape[2]
    n_pix, n_tm = lax.axis_size("pix"), lax.axis_size("tm")
    summed = lax.psum_scatter(partial_value, "pix", scatter_dimension=1, tiled=True)
    rows = summed.transpose(1, 0, 3, 2).reshape(K // n_pix, frames)
    moved = lax.all_to_all(rows, "tm", split_axis=0, concat_axis=1, tiled=True)
    here = moved.shape[0]
    start = (lax.axis_index("pix") * n_tm + lax.axis_index("tm")) * here
    widths = lax.dynamic_slice_in_dim(jnp.repeat(band_width, GROUP), start, here)
    nblocks = moved.shape[1] // FR
    padded = jnp.pad(moved.reshape(here, nblocks, FR), ((0, 0), (BMAX, BMAX), (0, 0)))
    filtered = jnp.zeros((here, nblocks, FR), jnp.float32)
    for d in range(2 * BMAX + 1):
        term = jnp.einsum(
            "kbf,fh->kbh", padded[:, d:d + nblocks], precision_blocks[d],
            preferred_element_type=jnp.float32,
        )
        filtered = filtered + jnp.where((abs(d - BMAX) <= widths)[:, None, None], term, 0.0)
    local = filtered.reshape(here, nblocks * FR).astype(jnp.bfloat16)
    traces = lax.all_to_all(local, "tm", split_axis=1, concat_axis=0, tiled=True)
    gathered = lax.all_gather(traces, "pix", axis=0, tiled=True)
    return rebuild(movie, footprints, block_ids, gathered)


def shards(movie, noise_weight, footprints, block_ids, band_width, precision_blocks):
    n_pix, n_tm = lax.axis_size("pix"), lax.axis_size("tm")
    tiles, slots, pixels, width = footprints.shape
    fits = movie.shape[2] == FR and n_pix == SIDE * SIDE and n_pix * n_tm == K // CBLK
    fits = fits and pixels == LANE and tiles * slots <= LANE and width == 4 * LANE
    rest = (movie, footprints, block_ids, band_width, precision_blocks)
    if fits:
        return middle(movie, noise_weight, *rest[1:])
    return middle_plain(project(movie, noise_weight, footprints, block_ids), *rest)


def solution(mesh):
    return jax.shard_map(
        shards,
        mesh=mesh,
        in_specs=(
            P("pix", None, "tm"),
            P("pix", None),
            P("pix", None, None, None),
            P("pix", None),
            P(),
            P(),
        ),
        out_specs=(P("pix", "tm"), P("pix", None, "tm")),
        check_vma=False,
    )
```

```python
import functools

import jax
import jax.numpy as jnp
from jax import lax
from jax.experimental import pallas as pl
from jax.experimental.pallas import tpu as pltpu
from jax.sharding import PartitionSpec as P

K = 16384
CBLK = 512
GROUP = 16
BMAX = 5
FR = 128
LANE = 128
SIDE = 2
HALVES = 2
SPLIT_SUM = (2, 2, 2, 1)
SPLIT_TRACE = (1, 2, 2, 2)
MESH = pl.DeviceIdType.MESH
VMEM_LIMIT = 56 * 1024 * 1024


def tile_batch(tiles):
    return 4 if tiles % 4 == 0 else 1


def project_kernel(ids_ref, movie_ref, noise_ref, feet_ref, out_ref, acc_ref):
    tile = pl.program_id(0)

    @pl.when(tile == 0)
    def _():
        acc_ref[...] = jnp.zeros_like(acc_ref)

    batch, slots = feet_ref.shape[:2]
    for member in range(batch):
        at = tile * batch + member
        pixels = movie_ref[member].astype(jnp.float32)
        weighted = (pixels.T * noise_ref[pl.ds(at, 1), :]).astype(jnp.bfloat16)
        products = [
            jnp.dot(weighted, feet_ref[member, slot], preferred_element_type=jnp.float32)
            for slot in range(slots)
        ]
        for slot in range(slots):
            acc_ref[ids_ref[at, slot]] += products[slot]

    @pl.when(tile == pl.num_programs(0) - 1)
    def _():
        def put(b, carry):
            for c in range(out_ref.shape[0]):
                span = slice(c * LANE, (c + 1) * LANE)
                out_ref[c, b] = acc_ref[b, :, span].astype(out_ref.dtype)
            return carry

        lax.fori_loop(0, out_ref.shape[1], put, 0)


def project(movie, noise_weight, footprints, block_ids):
    tiles, slots, pixels, width = footprints.shape
    frames = movie.shape[2]
    blocks = K // CBLK
    batch = tile_batch(tiles)
    shape = (width // LANE, blocks, frames, LANE)
    return pl.pallas_call(
        project_kernel,
        grid_spec=pltpu.PrefetchScalarGridSpec(
            num_scalar_prefetch=1,
            grid=(tiles // batch,),
            in_specs=[
                pl.BlockSpec((batch, pixels, frames), lambda n, ids: (n, 0, 0)),
                pl.BlockSpec((tiles, pixels), lambda n, ids: (0, 0)),
                pl.BlockSpec((batch, slots, pixels, width), lambda n, ids: (n, 0, 0, 0)),
            ],
            out_specs=pl.BlockSpec(shape, lambda n, ids: (0, 0, 0, 0)),
            scratch_shapes=[pltpu.VMEM((blocks, frames, width), jnp.float32)],
        ),
        out_shape=jax.ShapeDtypeStruct(shape, jnp.bfloat16),
        compiler_params=pltpu.CompilerParams(vmem_limit_bytes=VMEM_LIMIT),
        name="project",
    )(block_ids, movie, noise_weight, footprints)


def rebuild_kernel(ids_ref, me_ref, movie_ref, feet_ref, traces_ref, own_ref, out_ref):
    tile = pl.program_id(0)

    @pl.when(tile == 0)
    def _():
        count = own_ref.shape[0]

        def put(b, carry):
            own_ref[b] = traces_ref[me_ref[0] * count + b]
            return carry

        lax.fori_loop(0, count, put, 0)

    batch, slots = feet_ref.shape[:2]
    for member in range(batch):
        at = tile * batch + member
        rebuilt = None
        for slot in range(slots):
            term = jnp.dot(
                feet_ref[member, slot], traces_ref[ids_ref[at, slot]],
                preferred_element_type=jnp.float32,
            )
            rebuilt = term if rebuilt is None else rebuilt + term
        out_ref[member] = (movie_ref[member].astype(jnp.float32) - rebuilt).astype(out_ref.dtype)


def rebuild(movie, footprints, block_ids, traces):
    tiles, slots, pixels, width = footprints.shape
    frames = movie.shape[2]
    blocks = K // CBLK
    n_pix = lax.axis_size("pix")
    batch = tile_batch(tiles)
    own = (blocks // n_pix, width, frames)
    own_traces, residual = pl.pallas_call(
        rebuild_kernel,
        grid_spec=pltpu.PrefetchScalarGridSpec(
            num_scalar_prefetch=2,
            grid=(tiles // batch,),
            in_specs=[
                pl.BlockSpec((batch, pixels, frames), lambda n, ids, me: (n, 0, 0)),
                pl.BlockSpec((batch, slots, pixels, width), lambda n, ids, me: (n, 0, 0, 0)),
                pl.BlockSpec((blocks, width, frames), lambda n, ids, me: (0, 0, 0)),
            ],
            out_specs=[
                pl.BlockSpec(own, lambda n, ids, me: (0, 0, 0)),
                pl.BlockSpec((batch, pixels, frames), lambda n, ids, me: (n, 0, 0)),
            ],
        ),
        out_shape=[
            jax.ShapeDtypeStruct(own, jnp.bfloat16),
            jax.ShapeDtypeStruct(movie.shape, jnp.bfloat16),
        ],
        compiler_params=pltpu.CompilerParams(vmem_limit_bytes=VMEM_LIMIT),
        name="rebuild",
    )(
        block_ids, lax.axis_index("pix").reshape(1),
        movie, footprints, traces.reshape(blocks, width, frames),
    )
    return own_traces.reshape(K // n_pix, frames), residual


def middle_kernel(
    n_pix, n_tm, ids_hbm, band_hbm, noise_hbm, prec_hbm, movie_hbm, feet_hbm,
    traces_ref, residual_ref,
    far_buf, hop_out, in_buf, x_buf, xt_buf, y_buf,
    prec_t, feet_ref, total_ref, part_ref, sums_ref, weighted_ref,
    movie_ref, noise_ref, prec_ref, table_ref, table_smem, ids_ref, band_ref,
    far_r, in_r, g_r, b_r, a_r, relay_r, send_sem,
    feet_sem, piece_sem, movie_sem, small_sem, *gathered,
):
    chunks, tiles, slots = feet_ref.shape[:3]
    blocks = part_ref.shape[1]
    parts_half = n_tm // HALVES
    batch = tile_batch(tiles)
    pieces = tiles // batch
    nothing = tiles * slots
    me_p = lax.axis_index("pix")
    me_t = lax.axis_index("tm")
    me_x = lax.rem(me_p, SIDE)
    along_x = me_p + 1 - 2 * me_x
    along_y = lax.rem(me_p + SIDE, n_pix)
    across = lax.rem(along_x + SIDE, n_pix)
    first = (along_x, along_y)
    second = (along_y, along_x)

    far_first = sorted(range(1, n_tm), key=lambda e: abs(2 * e - n_tm))

    def tm_at(e):
        return lax.rem(me_t + e, n_tm)

    def part_at(owner, h):
        return pl.ds(owner * n_tm + h * parts_half, parts_half)

    barrier = pltpu.get_barrier_semaphore()
    for peer in first:
        pl.semaphore_signal(barrier, inc=1, device_id={"pix": peer}, device_id_type=MESH)
    for e in range(1, n_tm):
        pl.semaphore_signal(
            barrier, inc=1, device_id={"tm": tm_at(e)}, device_id_type=MESH
        )

    def feet_load(c, k):
        rows = pl.ds(k * batch, batch)
        return pltpu.make_async_copy(
            feet_hbm.at[rows, :, :, pl.ds(c * LANE, LANE)], feet_ref.at[c, rows],
            piece_sem.at[k] if c == 0 else feet_sem.at[c - 1],
        )

    def movie_load(k):
        rows = pl.ds(k * batch, batch)
        return pltpu.make_async_copy(movie_hbm.at[rows], movie_ref.at[rows], movie_sem.at[k])

    def arrived(ref, sem):
        pltpu.make_async_copy(ref, ref, sem).wait()

    load_ids = pltpu.make_async_copy(ids_hbm, ids_ref, small_sem.at[0])
    load_noise = pltpu.make_async_copy(noise_hbm, noise_ref, small_sem.at[1])
    load_prec = pltpu.make_async_copy(prec_hbm, prec_ref, small_sem.at[2])
    load_band = pltpu.make_async_copy(band_hbm, band_ref, small_sem.at[3])
    move_table = pltpu.make_async_copy(table_ref, table_smem, small_sem.at[4])

    load_ids.start()
    load_noise.start()
    for k in range(pieces):
        movie_load(k).start()
        feet_load(0, k).start()
    sums_ref[nothing] = jnp.zeros(sums_ref.shape[1:], sums_ref.dtype)
    load_ids.wait()

    lane = lax.broadcasted_iota(jnp.int32, (8, LANE), 1)

    def name_slots(n, row):
        for s in range(slots):
            row = jnp.where(lane == n * slots + s, ids_ref[s, n], row)
        return row

    named = lax.fori_loop(0, tiles, name_slots, jnp.zeros((8, LANE), jnp.int32))

    def link_slots(n, carry):
        prev, last = carry
        for s in range(slots):
            k = n * slots + s
            block = ids_ref[s, n]
            last = jnp.where(lane == block, k, last)
            prev = jnp.where((named == block) & (lane > k), k, prev)
        return prev, last

    start = jnp.full((8, LANE), nothing, jnp.int32)
    prev, last = lax.fori_loop(0, tiles, link_slots, (start, start))
    table_ref[0:8, :] = prev
    table_ref[8:16, :] = last
    move_table.start()
    load_noise.wait()
    move_table.wait()

    def project_chunk(c):
        if c > 0:
            arrived(feet_ref.at[c], feet_sem.at[c - 1])

        def step(k, carry):
            if c == 0:
                movie_load(k).wait()
                feet_load(c, k).wait()
            for member in range(batch):
                n = k * batch + member
                if c == 0:
                    pixels = movie_ref[n].astype(jnp.float32).T
                    weighted = (pixels * noise_ref[pl.ds(n, 1), :]).astype(jnp.bfloat16)
                    weighted_ref[n] = weighted
                else:
                    weighted = weighted_ref[n]
                feet = jnp.concatenate([feet_ref[c, n, s] for s in range(slots)], axis=1)
                products = jnp.dot(weighted, feet, preferred_element_type=jnp.float32)
                for s in range(slots):
                    at = n * slots + s
                    sums_ref[at] = sums_ref[table_smem[0, at]] + products[:, s * LANE:(s + 1) * LANE]
            return carry

        lax.fori_loop(0, pieces, step, 0)

    def put_parts(c, owner):
        for j in range(n_tm):
            b = owner * n_tm + j
            part_ref[c, b] = sums_ref[table_smem[8, b]].astype(part_ref.dtype)

    def put_rest(c):
        for owner in (across,) + first + (me_p,):
            put_parts(c, owner)

    def rows_at(split, c, u):
        size = FR // split[c]
        return pl.ds(u * size, size)

    def send_copy(source, target, sends, recv, axis, peer):
        return pltpu.make_async_remote_copy(
            src_ref=source, dst_ref=target, send_sem=send_sem.at[sends], recv_sem=recv,
            device_id={axis: peer}, device_id_type=MESH,
        )

    def far_copy(c, u, h):
        rows = rows_at(SPLIT_SUM, c, u)
        source = part_ref.at[c, part_at(across, h), rows]
        return send_copy(source, far_buf.at[c, h, :, rows], 0, far_r.at[c, u], "pix", first[h])

    def near_copy(c, u, h):
        rows = rows_at(SPLIT_SUM, c, u)
        source = part_ref.at[c, part_at(first[h], h), rows]
        return send_copy(source, in_buf.at[c, 0, h, :, rows], 0, in_r.at[c, u], "pix", first[h])

    def hop_copy(c, u, h):
        rows = rows_at(SPLIT_SUM, c, u)
        source = hop_out.at[c, h, :, rows]
        return send_copy(source, in_buf.at[c, 1, h, :, rows], 0, in_r.at[c, u], "pix", second[h])

    def g_copy(c, u, h):
        part = gathered[c].at[pl.ds(me_p * n_tm, n_tm), rows_at(SPLIT_TRACE, c, u)]
        return send_copy(part, part, 1, g_r.at[c, u], "pix", first[h])

    def relay_copy(c, u, h):
        part = gathered[c].at[part_at(first[h], h), rows_at(SPLIT_TRACE, c, u)]
        return send_copy(part, part, 0, relay_r.at[c], "pix", second[h])

    def a_copy(c, u, e):
        rows = rows_at(SPLIT_SUM, c, u)
        peer = tm_at(e)
        source = x_buf.at[c, peer, rows]
        return send_copy(source, xt_buf.at[c, me_t, rows], 1, a_r.at[c], "tm", peer)

    def b_copy(c, u, e):
        rows = rows_at(SPLIT_TRACE, c, u)
        peer = tm_at(e)
        target = gathered[c].at[me_p * n_tm + me_t, rows]
        return send_copy(y_buf.at[c, peer, rows], target, 1, b_r.at[c, u], "tm", peer)

    def send_far(c, u=0):
        for h in range(HALVES):
            far_copy(c, u, h).start()

    def send_near(c, u=0):
        for h in range(HALVES):
            near_copy(c, u, h).start()

    def send_hop(c, u=0):
        rows = rows_at(SPLIT_SUM, c, u)
        arrived(far_buf.at[c, :, :, rows], far_r.at[c, u])
        for h in range(HALVES):
            for g in range(parts_half):
                own = part_ref[c, second[h] * n_tm + h * parts_half + g, rows]
                total = own.astype(jnp.float32) + far_buf[c, h, g, rows].astype(jnp.float32)
                hop_out[c, h, g, rows] = total.astype(hop_out.dtype)
            hop_copy(c, u, h).start()

    def sum_chunk(c, u=0):
        rows = rows_at(SPLIT_SUM, c, u)
        arrived(in_buf.at[c, :, :, :, rows], in_r.at[c, u])
        for h in range(HALVES):
            for g in range(parts_half):
                part = h * parts_half + g
                total = part_ref[c, me_p * n_tm + part, rows].astype(jnp.float32)
                total = total + in_buf[c, 0, h, g, rows].astype(jnp.float32)
                total = total + in_buf[c, 1, h, g, rows].astype(jnp.float32)
                x_buf[c, part, rows] = total.astype(x_buf.dtype)
        for e in far_first:
            a_copy(c, u, e).start()
        xt_buf[c, me_t, rows] = x_buf[c, me_t, rows]

    def ready_filter():
        load_prec.wait()
        load_band.wait()
        for d in range(prec_ref.shape[0]):
            matrix = prec_ref[d].astype(jnp.float32)
            prec_t[:, d * FR:(d + 1) * FR] = matrix.T.astype(prec_t.dtype)

    def filter_chunk(c):
        groups = LANE // GROUP
        at = ((me_p * n_tm + me_t) * chunks + c) * groups
        column = lax.broadcasted_iota(jnp.int32, (1, LANE), 1)
        reach = jnp.zeros((1, LANE), jnp.int32)
        for g in range(groups):
            reach = jnp.where(column >= g * GROUP, band_ref[at + g], reach)
        keep = [
            jnp.where(reach >= k, 1.0, 0.0).astype(jnp.bfloat16) for k in range(BMAX + 1)
        ]
        arrived(xt_buf.at[c, pl.ds(0, n_tm - 1)], a_r.at[c])

        for i in range(n_tm):
            low, high = max(0, i - BMAX), min(n_tm, i + BMAX + 1)
            source = jnp.concatenate(
                [xt_buf[c, j] * keep[abs(j - i)] for j in range(low, high)], axis=0
            )
            bands = prec_t[:, (low - i + BMAX) * FR:(high - i + BMAX) * FR]
            result = jnp.dot(bands, source, preferred_element_type=jnp.float32)
            y_buf[c, i] = result.T.astype(jnp.bfloat16)

        for u in range(SPLIT_TRACE[c]):
            for e in far_first:
                b_copy(c, u, e).start()
        gathered[c][me_p * n_tm + me_t] = y_buf[c, me_t]

    def gather_chunk(c, u=0):
        rows = rows_at(SPLIT_TRACE, c, u)
        arrived(y_buf.at[c, pl.ds(0, n_tm - 1), rows], b_r.at[c, u])
        for h in range(HALVES):
            g_copy(c, u, h).start()
        size = FR // SPLIT_TRACE[c]
        span = slice(c * LANE + u * size, c * LANE + (u + 1) * size)
        for j in range(n_tm):
            traces_ref[j, span, :] = gathered[c][me_p * n_tm + j, rows]

    def relay_chunk(c, u=0):
        rows = rows_at(SPLIT_TRACE, c, u)
        arrived(gathered[c].at[pl.ds(0, HALVES * n_tm), rows], g_r.at[c, u])
        for h in range(HALVES):
            relay_copy(c, u, h).start()

    def rebuild_chunk(c):
        arrived(gathered[c].at[pl.ds(0, n_tm)], relay_r.at[c])

        def one_tile(n):
            feet = jnp.concatenate([feet_ref[c, n, s] for s in range(slots)], axis=1)
            chosen = jnp.concatenate(
                [gathered[c][ids_ref[s, n]] for s in range(slots)], axis=0
            )
            rebuilt = jnp.dot(feet, chosen, preferred_element_type=jnp.float32)
            if c > 0:
                rebuilt = rebuilt + total_ref[n]
            if c < chunks - 1:
                total_ref[n] = rebuilt
            else:
                left = movie_ref[n].astype(jnp.float32) - rebuilt
                residual_ref[n] = left.astype(residual_ref.dtype)

        def step(k, carry):
            for member in range(batch):
                one_tile(k * batch + member)
            return carry

        lax.fori_loop(0, pieces, step, 0)

    project_chunk(0)
    pl.semaphore_wait(barrier, len(first) + n_tm - 1)
    put_parts(0, across)
    send_far(0, 0)
    for peer in first:
        put_parts(0, peer)
    send_near(0, 0)
    send_far(0, 1)
    put_parts(0, me_p)
    load_prec.start()
    load_band.start()
    for c in range(1, chunks):
        for k in range(pieces):
            feet_load(c, k).start()
    project_chunk(1)
    put_rest(1)
    ready_filter()
    send_hop(0, 0)
    send_near(0, 1)
    send_far(1, 0)
    project_chunk(2)
    put_rest(2)
    send_hop(0, 1)
    sum_chunk(0, 0)
    send_near(1, 0)
    send_hop(1, 0)
    sum_chunk(0, 1)
    send_far(1, 1)
    send_near(1, 1)
    project_chunk(3)
    put_rest(3)
    send_far(2, 0)
    sum_chunk(1, 0)
    send_hop(1, 1)
    send_far(2, 1)
    send_near(2, 0)
    filter_chunk(0)
    send_hop(2, 0)
    send_far(3, 0)
    send_hop(2, 1)
    sum_chunk(1, 1)
    send_near(2, 1)
    send_hop(3, 0)
    sum_chunk(2, 0)
    send_near(3, 0)
    filter_chunk(1)
    gather_chunk(0, 0)
    gather_chunk(1, 0)
    sum_chunk(2, 1)
    sum_chunk(3, 0)
    gather_chunk(1, 1)
    relay_chunk(0, 0)
    filter_chunk(2)
    relay_chunk(1, 0)
    relay_chunk(1, 1)
    gather_chunk(2, 0)
    filter_chunk(3)
    gather_chunk(2, 1)
    relay_chunk(2, 0)
    gather_chunk(3, 0)
    rebuild_chunk(0)
    gather_chunk(3, 1)
    relay_chunk(2, 1)
    rebuild_chunk(1)
    relay_chunk(3, 0)
    relay_chunk(3, 1)
    rebuild_chunk(2)
    rebuild_chunk(3)
    arrived(part_ref, send_sem.at[0])
    arrived(part_ref.at[:, pl.ds(0, blocks - 2)], send_sem.at[1])


def finish_kernel(traces_ref, residual_ref, traces_hbm, residual_hbm, sem):
    copies = [
        pltpu.make_async_copy(traces_ref, traces_hbm, sem.at[0]),
        pltpu.make_async_copy(residual_ref, residual_hbm, sem.at[1]),
    ]
    for copy in copies:
        copy.start()
    for copy in copies:
        copy.wait()


def finish(traces, residual):
    hbm = pl.BlockSpec(memory_space=pl.ANY)
    vmem = pl.BlockSpec(memory_space=pltpu.VMEM)
    return pl.pallas_call(
        finish_kernel,
        out_shape=[
            jax.ShapeDtypeStruct(traces.shape, traces.dtype),
            jax.ShapeDtypeStruct(residual.shape, residual.dtype),
        ],
        in_specs=[vmem, vmem],
        out_specs=[hbm, hbm],
        scratch_shapes=[pltpu.SemaphoreType.DMA((2,))],
        name="finish",
    )(traces, residual)


def middle(movie, noise_weight, footprints, block_ids, band_width, precision_blocks):
    tiles, slots, pixels, width = footprints.shape
    frames = movie.shape[2]
    chunks, blocks, lanes = width // LANE, K // CBLK, LANE
    n_pix, n_tm = lax.axis_size("pix"), lax.axis_size("tm")
    pieces = tiles // tile_batch(tiles)
    dma = pltpu.SemaphoreType.DMA
    bf16, f32 = jnp.bfloat16, jnp.float32
    vmem = pl.BlockSpec(memory_space=pltpu.VMEM)
    part = (frames, lanes)
    traces, residual = pl.pallas_call(
        functools.partial(middle_kernel, n_pix, n_tm),
        out_shape=[
            pltpu.VMEM((n_tm, CBLK, frames), bf16),
            pltpu.VMEM(movie.shape, bf16),
        ],
        in_specs=[pl.BlockSpec(memory_space=pl.ANY)] * 6,
        out_specs=[vmem, vmem],
        scratch_shapes=[pltpu.VMEM((chunks, HALVES, n_tm // HALVES) + part, bf16)] * 2 + [
            pltpu.VMEM((chunks, 2, HALVES, n_tm // HALVES) + part, bf16),
            pltpu.VMEM((chunks, n_tm) + part, bf16),
            pltpu.VMEM((chunks, n_tm) + part, bf16),
            pltpu.VMEM((chunks, n_tm, lanes, frames), bf16),
            pltpu.VMEM((FR, precision_blocks.shape[0] * FR), bf16),
            pltpu.VMEM((chunks, tiles, slots, pixels, lanes), bf16),
            pltpu.VMEM(movie.shape, f32),
            pltpu.VMEM((chunks, blocks) + part, bf16),
            pltpu.VMEM((tiles * slots + 1,) + part, f32),
            pltpu.VMEM((tiles, frames, pixels), bf16),
            pltpu.VMEM(movie.shape, bf16),
            pltpu.VMEM(noise_weight.shape, f32),
            pltpu.VMEM(precision_blocks.shape, bf16),
            pltpu.VMEM((16, LANE), jnp.int32),
            pltpu.SMEM((16, LANE), jnp.int32),
            pltpu.SMEM((slots, tiles), jnp.int32),
            pltpu.SMEM(band_width.shape, jnp.int32),
        ] + [dma((chunks, 2))] * 4 + [dma((chunks,))] * 2 + [dma((2,))]
        + [dma((chunks - 1,)), dma((pieces,)), dma((pieces,)), dma((5,))]
        + [pltpu.VMEM((blocks, lanes, frames), bf16)] * chunks,
        compiler_params=pltpu.CompilerParams(
            collective_id=0, has_side_effects=True, vmem_limit_bytes=VMEM_LIMIT
        ),
        name="middle",
    )(block_ids.T, band_width, noise_weight, precision_blocks, movie, footprints)
    traces, residual = finish(
        pltpu.with_memory_space_constraint(traces, pltpu.VMEM),
        pltpu.with_memory_space_constraint(residual, pltpu.VMEM),
    )
    return traces.reshape(K // n_pix, frames), residual


def middle_plain(partial_value, movie, footprints, block_ids, band_width, precision_blocks):
    frames = movie.shape[2]
    n_pix, n_tm = lax.axis_size("pix"), lax.axis_size("tm")
    summed = lax.psum_scatter(partial_value, "pix", scatter_dimension=1, tiled=True)
    rows = summed.transpose(1, 0, 3, 2).reshape(K // n_pix, frames)
    moved = lax.all_to_all(rows, "tm", split_axis=0, concat_axis=1, tiled=True)
    here = moved.shape[0]
    start = (lax.axis_index("pix") * n_tm + lax.axis_index("tm")) * here
    widths = lax.dynamic_slice_in_dim(jnp.repeat(band_width, GROUP), start, here)
    nblocks = moved.shape[1] // FR
    padded = jnp.pad(moved.reshape(here, nblocks, FR), ((0, 0), (BMAX, BMAX), (0, 0)))
    filtered = jnp.zeros((here, nblocks, FR), jnp.float32)
    for d in range(2 * BMAX + 1):
        term = jnp.einsum(
            "kbf,fh->kbh", padded[:, d:d + nblocks], precision_blocks[d],
            preferred_element_type=jnp.float32,
        )
        filtered = filtered + jnp.where((abs(d - BMAX) <= widths)[:, None, None], term, 0.0)
    local = filtered.reshape(here, nblocks * FR).astype(jnp.bfloat16)
    traces = lax.all_to_all(local, "tm", split_axis=1, concat_axis=0, tiled=True)
    gathered = lax.all_gather(traces, "pix", axis=0, tiled=True)
    return rebuild(movie, footprints, block_ids, gathered)


def shards(movie, noise_weight, footprints, block_ids, band_width, precision_blocks):
    n_pix, n_tm = lax.axis_size("pix"), lax.axis_size("tm")
    tiles, slots, pixels, width = footprints.shape
    fits = movie.shape[2] == FR and n_pix == SIDE * SIDE and n_pix * n_tm == K // CBLK
    fits = fits and pixels == LANE and tiles * slots <= LANE and width == 4 * LANE
    rest = (movie, footprints, block_ids, band_width, precision_blocks)
    if fits:
        return middle(movie, noise_weight, *rest[1:])
    return middle_plain(project(movie, noise_weight, footprints, block_ids), *rest)


def solution(mesh):
    return jax.shard_map(
        shards,
        mesh=mesh,
        in_specs=(
            P("pix", None, "tm"),
            P("pix", None),
            P("pix", None, None, None),
            P("pix", None),
            P(),
            P(),
        ),
        out_specs=(P("pix", "tm"), P("pix", None, "tm")),
        check_vma=False,
    )
```

```python
import functools

import jax
import jax.numpy as jnp
from jax import lax
from jax.experimental import pallas as pl
from jax.experimental.pallas import tpu as pltpu
from jax.sharding import PartitionSpec as P

K = 16384
CBLK = 512
GROUP = 16
BMAX = 5
FR = 128
LANE = 128
SIDE = 2
HALVES = 2
SPLIT_SUM = (2, 2, 2, 1)
SPLIT_TRACE = (1, 2, 2, 2)
MESH = pl.DeviceIdType.MESH
VMEM_LIMIT = 56 * 1024 * 1024
MIDDLE_LIMIT = 42 * 1024 * 1024
FINISH_LIMIT = 8 * 1024 * 1024


def tile_batch(tiles):
    return 4 if tiles % 4 == 0 else 1


def project_kernel(ids_ref, movie_ref, noise_ref, feet_ref, out_ref, acc_ref):
    tile = pl.program_id(0)

    @pl.when(tile == 0)
    def _():
        acc_ref[...] = jnp.zeros_like(acc_ref)

    batch, slots = feet_ref.shape[:2]
    for member in range(batch):
        at = tile * batch + member
        pixels = movie_ref[member].astype(jnp.float32)
        weighted = (pixels.T * noise_ref[pl.ds(at, 1), :]).astype(jnp.bfloat16)
        products = [
            jnp.dot(weighted, feet_ref[member, slot], preferred_element_type=jnp.float32)
            for slot in range(slots)
        ]
        for slot in range(slots):
            acc_ref[ids_ref[at, slot]] += products[slot]

    @pl.when(tile == pl.num_programs(0) - 1)
    def _():
        def put(b, carry):
            for c in range(out_ref.shape[0]):
                span = slice(c * LANE, (c + 1) * LANE)
                out_ref[c, b] = acc_ref[b, :, span].astype(out_ref.dtype)
            return carry

        lax.fori_loop(0, out_ref.shape[1], put, 0)


def project(movie, noise_weight, footprints, block_ids):
    tiles, slots, pixels, width = footprints.shape
    frames = movie.shape[2]
    blocks = K // CBLK
    batch = tile_batch(tiles)
    shape = (width // LANE, blocks, frames, LANE)
    return pl.pallas_call(
        project_kernel,
        grid_spec=pltpu.PrefetchScalarGridSpec(
            num_scalar_prefetch=1,
            grid=(tiles // batch,),
            in_specs=[
                pl.BlockSpec((batch, pixels, frames), lambda n, ids: (n, 0, 0)),
                pl.BlockSpec((tiles, pixels), lambda n, ids: (0, 0)),
                pl.BlockSpec((batch, slots, pixels, width), lambda n, ids: (n, 0, 0, 0)),
            ],
            out_specs=pl.BlockSpec(shape, lambda n, ids: (0, 0, 0, 0)),
            scratch_shapes=[pltpu.VMEM((blocks, frames, width), jnp.float32)],
        ),
        out_shape=jax.ShapeDtypeStruct(shape, jnp.bfloat16),
        compiler_params=pltpu.CompilerParams(vmem_limit_bytes=VMEM_LIMIT),
        name="project",
    )(block_ids, movie, noise_weight, footprints)


def rebuild_kernel(ids_ref, me_ref, movie_ref, feet_ref, traces_ref, own_ref, out_ref):
    tile = pl.program_id(0)

    @pl.when(tile == 0)
    def _():
        count = own_ref.shape[0]

        def put(b, carry):
            own_ref[b] = traces_ref[me_ref[0] * count + b]
            return carry

        lax.fori_loop(0, count, put, 0)

    batch, slots = feet_ref.shape[:2]
    for member in range(batch):
        at = tile * batch + member
        rebuilt = None
        for slot in range(slots):
            term = jnp.dot(
                feet_ref[member, slot], traces_ref[ids_ref[at, slot]],
                preferred_element_type=jnp.float32,
            )
            rebuilt = term if rebuilt is None else rebuilt + term
        out_ref[member] = (movie_ref[member].astype(jnp.float32) - rebuilt).astype(out_ref.dtype)


def rebuild(movie, footprints, block_ids, traces):
    tiles, slots, pixels, width = footprints.shape
    frames = movie.shape[2]
    blocks = K // CBLK
    n_pix = lax.axis_size("pix")
    batch = tile_batch(tiles)
    own = (blocks // n_pix, width, frames)
    own_traces, residual = pl.pallas_call(
        rebuild_kernel,
        grid_spec=pltpu.PrefetchScalarGridSpec(
            num_scalar_prefetch=2,
            grid=(tiles // batch,),
            in_specs=[
                pl.BlockSpec((batch, pixels, frames), lambda n, ids, me: (n, 0, 0)),
                pl.BlockSpec((batch, slots, pixels, width), lambda n, ids, me: (n, 0, 0, 0)),
                pl.BlockSpec((blocks, width, frames), lambda n, ids, me: (0, 0, 0)),
            ],
            out_specs=[
                pl.BlockSpec(own, lambda n, ids, me: (0, 0, 0)),
                pl.BlockSpec((batch, pixels, frames), lambda n, ids, me: (n, 0, 0)),
            ],
        ),
        out_shape=[
            jax.ShapeDtypeStruct(own, jnp.bfloat16),
            jax.ShapeDtypeStruct(movie.shape, jnp.bfloat16),
        ],
        compiler_params=pltpu.CompilerParams(vmem_limit_bytes=VMEM_LIMIT),
        name="rebuild",
    )(
        block_ids, lax.axis_index("pix").reshape(1),
        movie, footprints, traces.reshape(blocks, width, frames),
    )
    return own_traces.reshape(K // n_pix, frames), residual


def middle_kernel(
    n_pix, n_tm, ids_hbm, band_hbm, noise_hbm, prec_hbm, movie_hbm, feet_hbm,
    traces_ref, base_ref, half_ref, chosen_ref,
    far_buf, hop_out, in_buf, x_buf, xt_buf, y_buf,
    prec_t, feet_ref, early_ref, part_ref, sums_ref, weighted_ref,
    movie_ref, noise_ref, prec_ref, table_ref, table_smem, ids_ref, band_ref,
    far_r, in_r, g_r, b_r, a_r, relay_r, send_sem,
    feet_sem, piece_sem, movie_sem, small_sem, *gathered,
):
    chunks, tiles, slots = feet_ref.shape[:3]
    blocks = part_ref.shape[1]
    parts_half = n_tm // HALVES
    batch = tile_batch(tiles)
    pieces = tiles // batch
    nothing = tiles * slots
    me_p = lax.axis_index("pix")
    me_t = lax.axis_index("tm")
    me_x = lax.rem(me_p, SIDE)
    along_x = me_p + 1 - 2 * me_x
    along_y = lax.rem(me_p + SIDE, n_pix)
    across = lax.rem(along_x + SIDE, n_pix)
    first = (along_x, along_y)
    second = (along_y, along_x)

    far_first = sorted(range(1, n_tm), key=lambda e: abs(2 * e - n_tm))

    def tm_at(e):
        return lax.rem(me_t + e, n_tm)

    def part_at(owner, h):
        return pl.ds(owner * n_tm + h * parts_half, parts_half)

    barrier = pltpu.get_barrier_semaphore()
    for peer in first:
        pl.semaphore_signal(barrier, inc=1, device_id={"pix": peer}, device_id_type=MESH)
    for e in range(1, n_tm):
        pl.semaphore_signal(
            barrier, inc=1, device_id={"tm": tm_at(e)}, device_id_type=MESH
        )

    def feet_load(c, k):
        rows = pl.ds(k * batch, batch)
        return pltpu.make_async_copy(
            feet_hbm.at[rows, :, :, pl.ds(c * LANE, LANE)], feet_ref.at[c, rows],
            piece_sem.at[k] if c == 0 else feet_sem.at[c - 1],
        )

    def movie_load(k):
        rows = pl.ds(k * batch, batch)
        return pltpu.make_async_copy(movie_hbm.at[rows], movie_ref.at[rows], movie_sem.at[k])

    def arrived(ref, sem):
        pltpu.make_async_copy(ref, ref, sem).wait()

    load_ids = pltpu.make_async_copy(ids_hbm, ids_ref, small_sem.at[0])
    load_noise = pltpu.make_async_copy(noise_hbm, noise_ref, small_sem.at[1])
    load_prec = pltpu.make_async_copy(prec_hbm, prec_ref, small_sem.at[2])
    load_band = pltpu.make_async_copy(band_hbm, band_ref, small_sem.at[3])
    move_table = pltpu.make_async_copy(table_ref, table_smem, small_sem.at[4])

    load_ids.start()
    load_noise.start()
    for k in range(pieces):
        movie_load(k).start()
        feet_load(0, k).start()
    sums_ref[nothing] = jnp.zeros(sums_ref.shape[1:], sums_ref.dtype)
    load_ids.wait()

    lane = lax.broadcasted_iota(jnp.int32, (8, LANE), 1)

    def name_slots(n, row):
        for s in range(slots):
            row = jnp.where(lane == n * slots + s, ids_ref[s, n], row)
        return row

    named = lax.fori_loop(0, tiles, name_slots, jnp.zeros((8, LANE), jnp.int32))

    def link_slots(n, carry):
        prev, last = carry
        for s in range(slots):
            k = n * slots + s
            block = ids_ref[s, n]
            last = jnp.where(lane == block, k, last)
            prev = jnp.where((named == block) & (lane > k), k, prev)
        return prev, last

    start = jnp.full((8, LANE), nothing, jnp.int32)
    prev, last = lax.fori_loop(0, tiles, link_slots, (start, start))
    table_ref[0:8, :] = prev
    table_ref[8:16, :] = last
    move_table.start()
    load_noise.wait()
    for k in range(pieces):
        movie_load(k).wait()
        for member in range(batch):
            n = k * batch + member
            pixels = movie_ref[n].astype(jnp.float32).T
            weighted_ref[n] = (pixels * noise_ref[n:n + 1, :]).astype(jnp.bfloat16)
    move_table.wait()

    def project_chunk(c):
        if c > 0:
            arrived(feet_ref.at[c], feet_sem.at[c - 1])

        def step(k, carry):
            if c == 0:
                feet_load(c, k).wait()
            for member in range(batch):
                n = k * batch + member
                feet = jnp.concatenate([feet_ref[c, n, s] for s in range(slots)], axis=1)
                products = jnp.dot(weighted_ref[n], feet, preferred_element_type=jnp.float32)
                before = [sums_ref[table_smem[0, n * slots + s]] for s in range(slots)]
                for s in range(slots):
                    sums_ref[n * slots + s] = before[s] + products[:, s * LANE:(s + 1) * LANE]
            return carry

        if c == 0:
            for k in range(pieces):
                step(k, 0)
        else:
            lax.fori_loop(0, pieces, step, 0)

    def put_parts(c, owner):
        for j in range(n_tm):
            b = owner * n_tm + j
            part_ref[c, b] = sums_ref[table_smem[8, b]].astype(part_ref.dtype)

    def put_rest(c):
        for owner in (across,) + first + (me_p,):
            put_parts(c, owner)

    def held(c, u):
        return gathered[sum(SPLIT_TRACE[:c]) + u]

    def rows_at(split, c, u):
        size = FR // split[c]
        return pl.ds(u * size, size)

    def send_copy(source, target, sends, recv, axis, peer):
        return pltpu.make_async_remote_copy(
            src_ref=source, dst_ref=target, send_sem=send_sem.at[sends], recv_sem=recv,
            device_id={axis: peer}, device_id_type=MESH,
        )

    def far_copy(c, u, h):
        rows = rows_at(SPLIT_SUM, c, u)
        source = part_ref.at[c, part_at(across, h), rows]
        return send_copy(source, far_buf.at[c, h, :, rows], 0, far_r.at[c, u], "pix", first[h])

    def near_copy(c, u, h):
        rows = rows_at(SPLIT_SUM, c, u)
        source = part_ref.at[c, part_at(first[h], h), rows]
        return send_copy(source, in_buf.at[c, 0, h, :, rows], 0, in_r.at[c, u], "pix", first[h])

    def hop_copy(c, u, h):
        rows = rows_at(SPLIT_SUM, c, u)
        source = hop_out.at[c, h, :, rows]
        return send_copy(source, in_buf.at[c, 1, h, :, rows], 0, in_r.at[c, u], "pix", second[h])

    def g_copy(c, u, h):
        part = held(c, u).at[pl.ds(me_p * n_tm, n_tm)]
        return send_copy(part, part, 1, g_r.at[c, u], "pix", first[h])

    def relay_copy(c, u, h):
        part = held(c, u).at[part_at(first[h], h)]
        return send_copy(part, part, 0, relay_r.at[c, u], "pix", second[h])

    def a_copy(c, u, e):
        rows = rows_at(SPLIT_SUM, c, u)
        peer = tm_at(e)
        source = x_buf.at[c, peer, rows]
        return send_copy(source, xt_buf.at[c, me_t, rows], 1, a_r.at[c], "tm", peer)

    def b_copy(c, u, e):
        rows = rows_at(SPLIT_TRACE, c, u)
        peer = tm_at(e)
        target = held(c, u).at[me_p * n_tm + me_t]
        return send_copy(y_buf.at[c, peer, rows], target, 1, b_r.at[c, u], "tm", peer)

    def send_far(c, u=0):
        for h in range(HALVES):
            far_copy(c, u, h).start()

    def send_near(c, u=0):
        for h in range(HALVES):
            near_copy(c, u, h).start()

    def send_hop(c, u=0):
        rows = rows_at(SPLIT_SUM, c, u)
        arrived(far_buf.at[c, :, :, rows], far_r.at[c, u])
        for h in range(HALVES):
            for g in range(parts_half):
                own = part_ref[c, second[h] * n_tm + h * parts_half + g, rows]
                total = own.astype(jnp.float32) + far_buf[c, h, g, rows].astype(jnp.float32)
                hop_out[c, h, g, rows] = total.astype(hop_out.dtype)
            hop_copy(c, u, h).start()

    def sum_chunk(c, u=0):
        rows = rows_at(SPLIT_SUM, c, u)
        arrived(in_buf.at[c, :, :, :, rows], in_r.at[c, u])
        for h in range(HALVES):
            for g in range(parts_half):
                part = h * parts_half + g
                total = part_ref[c, me_p * n_tm + part, rows].astype(jnp.float32)
                total = total + in_buf[c, 0, h, g, rows].astype(jnp.float32)
                total = total + in_buf[c, 1, h, g, rows].astype(jnp.float32)
                x_buf[c, part, rows] = total.astype(x_buf.dtype)
        for e in far_first:
            a_copy(c, u, e).start()
        xt_buf[c, me_t, rows] = x_buf[c, me_t, rows]

    def ready_filter():
        load_prec.wait()
        load_band.wait()
        for d in range(prec_ref.shape[0]):
            matrix = prec_ref[d].astype(jnp.float32)
            prec_t[:, d * FR:(d + 1) * FR] = matrix.T.astype(prec_t.dtype)

    def filter_chunk(c):
        groups = LANE // GROUP
        at = ((me_p * n_tm + me_t) * chunks + c) * groups
        column = lax.broadcasted_iota(jnp.int32, (1, LANE), 1)
        reach = jnp.zeros((1, LANE), jnp.int32)
        for g in range(groups):
            reach = jnp.where(column >= g * GROUP, band_ref[at + g], reach)
        keep = [
            jnp.where(reach >= k, 1.0, 0.0).astype(jnp.bfloat16) for k in range(BMAX + 1)
        ]
        arrived(xt_buf.at[c, pl.ds(0, n_tm - 1)], a_r.at[c])

        for i in range(n_tm):
            low, high = max(0, i - BMAX), min(n_tm, i + BMAX + 1)
            source = jnp.concatenate(
                [xt_buf[c, j] * keep[abs(j - i)] for j in range(low, high)], axis=0
            )
            bands = prec_t[:, (low - i + BMAX) * FR:(high - i + BMAX) * FR]
            result = jnp.dot(bands, source, preferred_element_type=jnp.float32)
            y_buf[c, i] = result.T.astype(jnp.bfloat16)

        for u in range(SPLIT_TRACE[c]):
            for e in far_first:
                b_copy(c, u, e).start()
        for u in range(SPLIT_TRACE[c]):
            held(c, u)[me_p * n_tm + me_t] = y_buf[c, me_t, rows_at(SPLIT_TRACE, c, u)]

    def gather_chunk(c, u=0):
        rows = rows_at(SPLIT_TRACE, c, u)
        arrived(y_buf.at[c, pl.ds(0, n_tm - 1), rows], b_r.at[c, u])
        for h in range(HALVES):
            g_copy(c, u, h).start()
        size = FR // SPLIT_TRACE[c]
        span = slice(c * LANE + u * size, c * LANE + (u + 1) * size)
        for j in range(n_tm):
            traces_ref[j, span, :] = held(c, u)[me_p * n_tm + j]

    def relay_chunk(c, u=0):
        arrived(held(c, u).at[pl.ds(0, HALVES * n_tm)], g_r.at[c, u])
        for h in range(HALVES):
            relay_copy(c, u, h).start()

    def each_tile(one_tile):
        def step(k, carry):
            for member in range(batch):
                one_tile(k * batch + member)
            return carry

        lax.fori_loop(0, pieces, step, 0)

    def rebuild_chunk(c):
        for u in range(SPLIT_TRACE[c]):
            arrived(held(c, u).at[pl.ds(0, n_tm)], relay_r.at[c, u])

        def one_tile(n):
            feet = jnp.concatenate([feet_ref[c, n, s] for s in range(slots)], axis=1)
            chosen = jnp.concatenate(
                [
                    held(c, u)[ids_ref[s, n]]
                    for s in range(slots) for u in range(SPLIT_TRACE[c])
                ],
                axis=0,
            )
            rebuilt = jnp.dot(feet, chosen, preferred_element_type=jnp.float32)
            before = base_ref[n] if c > 0 else movie_ref[n].astype(jnp.float32)
            base_ref[n] = before - rebuilt

        each_tile(one_tile)

    half = LANE // 2

    def split_feet():
        def one_tile(n):
            for u, target in ((0, early_ref), (1, half_ref)):
                span = slice(u * half, (u + 1) * half)
                target[n] = jnp.concatenate(
                    [feet_ref[chunks - 1, n, s][:, span] for s in range(slots)], axis=1
                )

        each_tile(one_tile)

    def choose(n, u):
        return jnp.concatenate(
            [held(chunks - 1, u)[ids_ref[s, n]] for s in range(slots)], axis=0
        )

    def rebuild_early():
        arrived(held(chunks - 1, 0).at[pl.ds(0, n_tm)], relay_r.at[chunks - 1, 0])

        def one_tile(n):
            rebuilt = jnp.dot(early_ref[n], choose(n, 0), preferred_element_type=jnp.float32)
            base_ref[n] = base_ref[n] - rebuilt

        each_tile(one_tile)

    def choose_late():
        arrived(held(chunks - 1, 1).at[pl.ds(0, n_tm)], relay_r.at[chunks - 1, 1])

        def one_tile(n):
            chosen_ref[n] = choose(n, 1)

        each_tile(one_tile)

    project_chunk(0)
    pl.semaphore_wait(barrier, len(first) + n_tm - 1)
    put_parts(0, across)
    send_far(0, 0)
    for peer in first:
        put_parts(0, peer)
    send_near(0, 0)
    send_far(0, 1)
    put_parts(0, me_p)
    load_prec.start()
    load_band.start()
    for c in range(1, chunks):
        for k in range(pieces):
            feet_load(c, k).start()
    project_chunk(1)
    put_rest(1)
    ready_filter()
    send_hop(0, 0)
    send_near(0, 1)
    send_far(1, 0)
    project_chunk(2)
    put_rest(2)
    send_hop(0, 1)
    sum_chunk(0, 0)
    send_near(1, 0)
    send_hop(1, 0)
    sum_chunk(0, 1)
    send_far(1, 1)
    send_near(1, 1)
    project_chunk(3)
    put_rest(3)
    send_far(2, 0)
    sum_chunk(1, 0)
    send_hop(1, 1)
    send_far(2, 1)
    send_near(2, 0)
    filter_chunk(0)
    send_hop(2, 0)
    send_far(3, 0)
    send_hop(2, 1)
    sum_chunk(1, 1)
    send_near(2, 1)
    send_hop(3, 0)
    sum_chunk(2, 0)
    send_near(3, 0)
    filter_chunk(1)
    gather_chunk(0, 0)
    gather_chunk(1, 0)
    sum_chunk(2, 1)
    sum_chunk(3, 0)
    gather_chunk(1, 1)
    relay_chunk(0, 0)
    filter_chunk(2)
    relay_chunk(1, 0)
    relay_chunk(1, 1)
    gather_chunk(2, 0)
    filter_chunk(3)
    split_feet()
    gather_chunk(2, 1)
    relay_chunk(2, 0)
    gather_chunk(3, 0)
    rebuild_chunk(0)
    gather_chunk(3, 1)
    relay_chunk(2, 1)
    rebuild_chunk(1)
    relay_chunk(3, 0)
    relay_chunk(3, 1)
    rebuild_chunk(2)
    rebuild_early()
    choose_late()
    arrived(part_ref, send_sem.at[0])
    arrived(part_ref.at[:, pl.ds(0, blocks - 2)], send_sem.at[1])


def finish_kernel(
    traces_ref, base_ref, half_ref, chosen_ref, traces_hbm, residual_hbm, residual_ref, sem
):
    tiles = base_ref.shape[0]
    batch = tile_batch(tiles)
    copies = [pltpu.make_async_copy(traces_ref, traces_hbm, sem.at[0])]
    copies[0].start()
    for k in range(tiles // batch):
        for member in range(batch):
            n = k * batch + member
            rebuilt = jnp.dot(half_ref[n], chosen_ref[n], preferred_element_type=jnp.float32)
            residual_ref[n] = (base_ref[n] - rebuilt).astype(residual_ref.dtype)
        rows = pl.ds(k * batch, batch)
        copies.append(
            pltpu.make_async_copy(residual_ref.at[rows], residual_hbm.at[rows], sem.at[k + 1])
        )
        copies[-1].start()
    for copy in copies:
        copy.wait()


def finish(traces, base, half, chosen):
    hbm = pl.BlockSpec(memory_space=pl.ANY)
    vmem = pl.BlockSpec(memory_space=pltpu.VMEM)
    held = [
        pltpu.with_memory_space_constraint(x, pltpu.VMEM) for x in (traces, base, half, chosen)
    ]
    tiles = base.shape[0]
    return pl.pallas_call(
        finish_kernel,
        out_shape=[
            jax.ShapeDtypeStruct(traces.shape, jnp.bfloat16),
            jax.ShapeDtypeStruct(base.shape, jnp.bfloat16),
        ],
        in_specs=[vmem] * 4,
        out_specs=[hbm, hbm],
        scratch_shapes=[
            pltpu.VMEM(base.shape, jnp.bfloat16),
            pltpu.SemaphoreType.DMA((tiles // tile_batch(tiles) + 1,)),
        ],
        compiler_params=pltpu.CompilerParams(vmem_limit_bytes=FINISH_LIMIT),
        name="finish",
    )(*held)


def middle(movie, noise_weight, footprints, block_ids, band_width, precision_blocks):
    tiles, slots, pixels, width = footprints.shape
    frames = movie.shape[2]
    chunks, blocks, lanes = width // LANE, K // CBLK, LANE
    n_pix, n_tm = lax.axis_size("pix"), lax.axis_size("tm")
    pieces = tiles // tile_batch(tiles)
    dma = pltpu.SemaphoreType.DMA
    bf16, f32 = jnp.bfloat16, jnp.float32
    vmem = pl.BlockSpec(memory_space=pltpu.VMEM)
    part = (frames, lanes)
    operands = (block_ids.T, band_width, noise_weight, precision_blocks, movie, footprints)
    parts = pl.pallas_call(
        functools.partial(middle_kernel, n_pix, n_tm),
        out_shape=[
            pltpu.VMEM((n_tm, CBLK, frames), bf16),
            pltpu.VMEM(movie.shape, f32),
            pltpu.VMEM((tiles, pixels, slots * lanes // 2), bf16),
            pltpu.VMEM((tiles, slots * lanes // 2, frames), bf16),
        ],
        in_specs=[pl.BlockSpec(memory_space=pl.ANY)] * 6,
        out_specs=[vmem] * 4,
        scratch_shapes=[pltpu.VMEM((chunks, HALVES, n_tm // HALVES) + part, bf16)] * 2 + [
            pltpu.VMEM((chunks, 2, HALVES, n_tm // HALVES) + part, bf16),
            pltpu.VMEM((chunks, n_tm) + part, bf16),
            pltpu.VMEM((chunks, n_tm) + part, bf16),
            pltpu.VMEM((chunks, n_tm, lanes, frames), bf16),
            pltpu.VMEM((FR, precision_blocks.shape[0] * FR), bf16),
            pltpu.VMEM((chunks, tiles, slots, pixels, lanes), bf16),
            pltpu.VMEM((tiles, pixels, slots * lanes // 2), bf16),
            pltpu.VMEM((chunks, blocks) + part, bf16),
            pltpu.VMEM((tiles * slots + 1,) + part, f32),
            pltpu.VMEM((tiles, frames, pixels), bf16),
            pltpu.VMEM(movie.shape, bf16),
            pltpu.VMEM(noise_weight.shape, f32),
            pltpu.VMEM(precision_blocks.shape, bf16),
            pltpu.VMEM((16, LANE), jnp.int32),
            pltpu.SMEM((16, LANE), jnp.int32),
            pltpu.SMEM((slots, tiles), jnp.int32),
            pltpu.SMEM(band_width.shape, jnp.int32),
        ] + [dma((chunks, 2))] * 4 + [dma((chunks,)), dma((chunks, 2)), dma((2,))]
        + [dma((chunks - 1,)), dma((pieces,)), dma((pieces,)), dma((5,))]
        + [pltpu.VMEM((blocks, lanes // n, frames), bf16) for n in SPLIT_TRACE for _ in range(n)],
        compiler_params=pltpu.CompilerParams(
            collective_id=0, has_side_effects=True, vmem_limit_bytes=MIDDLE_LIMIT
        ),
        name="middle",
    )(*[pltpu.with_memory_space_constraint(x, pltpu.HBM) for x in operands])
    traces, residual = finish(*parts)
    return traces.reshape(K // n_pix, frames), residual


def middle_plain(partial_value, movie, footprints, block_ids, band_width, precision_blocks):
    frames = movie.shape[2]
    n_pix, n_tm = lax.axis_size("pix"), lax.axis_size("tm")
    summed = lax.psum_scatter(partial_value, "pix", scatter_dimension=1, tiled=True)
    rows = summed.transpose(1, 0, 3, 2).reshape(K // n_pix, frames)
    moved = lax.all_to_all(rows, "tm", split_axis=0, concat_axis=1, tiled=True)
    here = moved.shape[0]
    start = (lax.axis_index("pix") * n_tm + lax.axis_index("tm")) * here
    widths = lax.dynamic_slice_in_dim(jnp.repeat(band_width, GROUP), start, here)
    nblocks = moved.shape[1] // FR
    padded = jnp.pad(moved.reshape(here, nblocks, FR), ((0, 0), (BMAX, BMAX), (0, 0)))
    filtered = jnp.zeros((here, nblocks, FR), jnp.float32)
    for d in range(2 * BMAX + 1):
        term = jnp.einsum(
            "kbf,fh->kbh", padded[:, d:d + nblocks], precision_blocks[d],
            preferred_element_type=jnp.float32,
        )
        filtered = filtered + jnp.where((abs(d - BMAX) <= widths)[:, None, None], term, 0.0)
    local = filtered.reshape(here, nblocks * FR).astype(jnp.bfloat16)
    traces = lax.all_to_all(local, "tm", split_axis=1, concat_axis=0, tiled=True)
    gathered = lax.all_gather(traces, "pix", axis=0, tiled=True)
    return rebuild(movie, footprints, block_ids, gathered)


def shards(movie, noise_weight, footprints, block_ids, band_width, precision_blocks):
    n_pix, n_tm = lax.axis_size("pix"), lax.axis_size("tm")
    tiles, slots, pixels, width = footprints.shape
    fits = movie.shape[2] == FR and n_pix == SIDE * SIDE and n_pix * n_tm == K // CBLK
    fits = fits and pixels == LANE and tiles * slots <= LANE and width == 4 * LANE
    rest = (movie, footprints, block_ids, band_width, precision_blocks)
    if fits:
        return middle(movie, noise_weight, *rest[1:])
    return middle_plain(project(movie, noise_weight, footprints, block_ids), *rest)


def solution(mesh):
    return jax.shard_map(
        shards,
        mesh=mesh,
        in_specs=(
            P("pix", None, "tm"),
            P("pix", None),
            P("pix", None, None, None),
            P("pix", None),
            P(),
            P(),
        ),
        out_specs=(P("pix", "tm"), P("pix", None, "tm")),
        check_vma=False,
    )
```

```python
import functools

import jax
import jax.numpy as jnp
from jax import lax
from jax.experimental import pallas as pl
from jax.experimental.pallas import tpu as pltpu
from jax.sharding import PartitionSpec as P

K = 16384
CBLK = 512
GROUP = 16
BMAX = 5
FR = 128
LANE = 128
SIDE = 2
HALVES = 2
SPLIT_SUM = (2, 2, 2, 1)
SPLIT_TRACE = (1, 1, 2, 2)
MESH = pl.DeviceIdType.MESH
VMEM_LIMIT = 56 * 1024 * 1024
MIDDLE_LIMIT = 42 * 1024 * 1024
FINISH_LIMIT = 8 * 1024 * 1024


def tile_batch(tiles):
    return 4 if tiles % 4 == 0 else 1


def project_kernel(ids_ref, movie_ref, noise_ref, feet_ref, out_ref, acc_ref):
    tile = pl.program_id(0)

    @pl.when(tile == 0)
    def _():
        acc_ref[...] = jnp.zeros_like(acc_ref)

    batch, slots = feet_ref.shape[:2]
    for member in range(batch):
        at = tile * batch + member
        pixels = movie_ref[member].astype(jnp.float32)
        weighted = (pixels.T * noise_ref[pl.ds(at, 1), :]).astype(jnp.bfloat16)
        products = [
            jnp.dot(weighted, feet_ref[member, slot], preferred_element_type=jnp.float32)
            for slot in range(slots)
        ]
        for slot in range(slots):
            acc_ref[ids_ref[at, slot]] += products[slot]

    @pl.when(tile == pl.num_programs(0) - 1)
    def _():
        def put(b, carry):
            for c in range(out_ref.shape[0]):
                span = slice(c * LANE, (c + 1) * LANE)
                out_ref[c, b] = acc_ref[b, :, span].astype(out_ref.dtype)
            return carry

        lax.fori_loop(0, out_ref.shape[1], put, 0)


def project(movie, noise_weight, footprints, block_ids):
    tiles, slots, pixels, width = footprints.shape
    frames = movie.shape[2]
    blocks = K // CBLK
    batch = tile_batch(tiles)
    shape = (width // LANE, blocks, frames, LANE)
    return pl.pallas_call(
        project_kernel,
        grid_spec=pltpu.PrefetchScalarGridSpec(
            num_scalar_prefetch=1,
            grid=(tiles // batch,),
            in_specs=[
                pl.BlockSpec((batch, pixels, frames), lambda n, ids: (n, 0, 0)),
                pl.BlockSpec((tiles, pixels), lambda n, ids: (0, 0)),
                pl.BlockSpec((batch, slots, pixels, width), lambda n, ids: (n, 0, 0, 0)),
            ],
            out_specs=pl.BlockSpec(shape, lambda n, ids: (0, 0, 0, 0)),
            scratch_shapes=[pltpu.VMEM((blocks, frames, width), jnp.float32)],
        ),
        out_shape=jax.ShapeDtypeStruct(shape, jnp.bfloat16),
        compiler_params=pltpu.CompilerParams(vmem_limit_bytes=VMEM_LIMIT),
        name="project",
    )(block_ids, movie, noise_weight, footprints)


def rebuild_kernel(ids_ref, me_ref, movie_ref, feet_ref, traces_ref, own_ref, out_ref):
    tile = pl.program_id(0)

    @pl.when(tile == 0)
    def _():
        count = own_ref.shape[0]

        def put(b, carry):
            own_ref[b] = traces_ref[me_ref[0] * count + b]
            return carry

        lax.fori_loop(0, count, put, 0)

    batch, slots = feet_ref.shape[:2]
    for member in range(batch):
        at = tile * batch + member
        rebuilt = None
        for slot in range(slots):
            term = jnp.dot(
                feet_ref[member, slot], traces_ref[ids_ref[at, slot]],
                preferred_element_type=jnp.float32,
            )
            rebuilt = term if rebuilt is None else rebuilt + term
        out_ref[member] = (movie_ref[member].astype(jnp.float32) - rebuilt).astype(out_ref.dtype)


def rebuild(movie, footprints, block_ids, traces):
    tiles, slots, pixels, width = footprints.shape
    frames = movie.shape[2]
    blocks = K // CBLK
    n_pix = lax.axis_size("pix")
    batch = tile_batch(tiles)
    own = (blocks // n_pix, width, frames)
    own_traces, residual = pl.pallas_call(
        rebuild_kernel,
        grid_spec=pltpu.PrefetchScalarGridSpec(
            num_scalar_prefetch=2,
            grid=(tiles // batch,),
            in_specs=[
                pl.BlockSpec((batch, pixels, frames), lambda n, ids, me: (n, 0, 0)),
                pl.BlockSpec((batch, slots, pixels, width), lambda n, ids, me: (n, 0, 0, 0)),
                pl.BlockSpec((blocks, width, frames), lambda n, ids, me: (0, 0, 0)),
            ],
            out_specs=[
                pl.BlockSpec(own, lambda n, ids, me: (0, 0, 0)),
                pl.BlockSpec((batch, pixels, frames), lambda n, ids, me: (n, 0, 0)),
            ],
        ),
        out_shape=[
            jax.ShapeDtypeStruct(own, jnp.bfloat16),
            jax.ShapeDtypeStruct(movie.shape, jnp.bfloat16),
        ],
        compiler_params=pltpu.CompilerParams(vmem_limit_bytes=VMEM_LIMIT),
        name="rebuild",
    )(
        block_ids, lax.axis_index("pix").reshape(1),
        movie, footprints, traces.reshape(blocks, width, frames),
    )
    return own_traces.reshape(K // n_pix, frames), residual


def middle_kernel(
    n_pix, n_tm, ids_hbm, band_hbm, noise_hbm, prec_hbm, movie_hbm, feet_hbm,
    traces_ref, base_ref, half_ref, chosen_ref,
    far_buf, hop_out, in_buf, x_buf, xt_buf, y_buf,
    prec_t, feet_ref, early_ref, part_ref, sums_ref, weighted_ref,
    movie_ref, noise_ref, prec_ref, table_ref, table_smem, ids_ref, band_ref,
    far_r, in_r, g_r, b_r, a_r, relay_r, send_sem,
    feet_sem, piece_sem, movie_sem, small_sem, *gathered,
):
    chunks, tiles, slots = feet_ref.shape[:3]
    blocks = part_ref.shape[1]
    parts_half = n_tm // HALVES
    batch = tile_batch(tiles)
    pieces = tiles // batch
    nothing = tiles * slots
    me_p = lax.axis_index("pix")
    me_t = lax.axis_index("tm")
    me_x = lax.rem(me_p, SIDE)
    along_x = me_p + 1 - 2 * me_x
    along_y = lax.rem(me_p + SIDE, n_pix)
    across = lax.rem(along_x + SIDE, n_pix)
    first = (along_x, along_y)
    second = (along_y, along_x)

    far_first = sorted(range(1, n_tm), key=lambda e: abs(2 * e - n_tm))

    def tm_at(e):
        return lax.rem(me_t + e, n_tm)

    def part_at(owner, h):
        return pl.ds(owner * n_tm + h * parts_half, parts_half)

    barrier = pltpu.get_barrier_semaphore()
    for peer in first:
        pl.semaphore_signal(barrier, inc=1, device_id={"pix": peer}, device_id_type=MESH)
    for e in range(1, n_tm):
        pl.semaphore_signal(
            barrier, inc=1, device_id={"tm": tm_at(e)}, device_id_type=MESH
        )

    def feet_load(c, k):
        rows = pl.ds(k * batch, batch)
        return pltpu.make_async_copy(
            feet_hbm.at[rows, :, :, pl.ds(c * LANE, LANE)], feet_ref.at[c, rows],
            piece_sem.at[k] if c == 0 else feet_sem.at[c - 1],
        )

    def movie_load(k):
        rows = pl.ds(k * batch, batch)
        return pltpu.make_async_copy(movie_hbm.at[rows], movie_ref.at[rows], movie_sem.at[k])

    def arrived(ref, sem):
        pltpu.make_async_copy(ref, ref, sem).wait()

    load_ids = pltpu.make_async_copy(ids_hbm, ids_ref, small_sem.at[0])
    load_noise = pltpu.make_async_copy(noise_hbm, noise_ref, small_sem.at[1])
    load_prec = pltpu.make_async_copy(prec_hbm, prec_ref, small_sem.at[2])
    load_band = pltpu.make_async_copy(band_hbm, band_ref, small_sem.at[3])
    move_table = pltpu.make_async_copy(table_ref, table_smem, small_sem.at[4])

    load_ids.start()
    load_noise.start()
    for k in range(pieces):
        movie_load(k).start()
        feet_load(0, k).start()
    sums_ref[nothing] = jnp.zeros(sums_ref.shape[1:], sums_ref.dtype)
    load_ids.wait()

    lane = lax.broadcasted_iota(jnp.int32, (8, LANE), 1)

    named = jnp.zeros((8, LANE), jnp.int32)
    for k in range(nothing):
        named = jnp.where(lane == k, ids_ref[k % slots, k // slots], named)
    prev = jnp.full((8, LANE), nothing, jnp.int32)
    last = prev
    for k in range(nothing):
        block = ids_ref[k % slots, k // slots]
        last = jnp.where(lane == block, k, last)
        prev = jnp.where((named == block) & (lane > k), k, prev)
    table_ref[0:8, :] = prev
    table_ref[8:16, :] = last
    move_table.start()
    load_noise.wait()
    for k in range(pieces):
        movie_load(k).wait()
        for member in range(batch):
            n = k * batch + member
            pixels = movie_ref[n].astype(jnp.float32).T
            weighted_ref[n] = (pixels * noise_ref[n:n + 1, :]).astype(jnp.bfloat16)
    move_table.wait()

    def one_tile(n, c, rows):
        feet = jnp.concatenate([feet_ref[c, n, s] for s in range(slots)], axis=1)
        products = jnp.dot(weighted_ref[n, rows], feet, preferred_element_type=jnp.float32)
        before = [sums_ref[table_smem[0, n * slots + s], rows] for s in range(slots)]
        for s in range(slots):
            total = before[s] + products[:, s * LANE:(s + 1) * LANE]
            sums_ref[n * slots + s, rows] = total

    def project_chunk(c):
        arrived(feet_ref.at[c], feet_sem.at[c - 1])

        def step(k, carry):
            for member in range(batch):
                one_tile(k * batch + member, c, slice(0, FR))
            return carry

        lax.fori_loop(0, pieces, step, 0)

    def project_part(u):
        size = FR // SPLIT_SUM[0]
        for n in range(tiles):
            if u == 0 and n % batch == 0:
                feet_load(0, n // batch).wait()
            one_tile(n, 0, slice(u * size, (u + 1) * size))

    def put_parts(c, owner, rows=slice(0, FR)):
        for j in range(n_tm):
            b = owner * n_tm + j
            part_ref[c, b, rows] = sums_ref[table_smem[8, b], rows].astype(part_ref.dtype)

    def put_rest(c):
        for owner in (across,) + first + (me_p,):
            put_parts(c, owner)

    def held(c, u):
        return gathered[sum(SPLIT_TRACE[:c]) + u]

    def rows_at(split, c, u):
        size = FR // split[c]
        return pl.ds(u * size, size)

    def send_copy(source, target, sends, recv, axis, peer):
        return pltpu.make_async_remote_copy(
            src_ref=source, dst_ref=target, send_sem=send_sem.at[sends], recv_sem=recv,
            device_id={axis: peer}, device_id_type=MESH,
        )

    def far_copy(c, u, h):
        rows = rows_at(SPLIT_SUM, c, u)
        source = part_ref.at[c, part_at(across, h), rows]
        return send_copy(source, far_buf.at[c, h, :, rows], 0, far_r.at[c, u], "pix", first[h])

    def near_copy(c, u, h):
        rows = rows_at(SPLIT_SUM, c, u)
        source = part_ref.at[c, part_at(first[h], h), rows]
        return send_copy(source, in_buf.at[c, 0, h, :, rows], 0, in_r.at[c, u], "pix", first[h])

    def hop_copy(c, u, h):
        rows = rows_at(SPLIT_SUM, c, u)
        source = hop_out.at[c, h, :, rows]
        return send_copy(source, in_buf.at[c, 1, h, :, rows], 0, in_r.at[c, u], "pix", second[h])

    def g_copy(c, u, h):
        part = held(c, u).at[pl.ds(me_p * n_tm, n_tm)]
        return send_copy(part, part, 1, g_r.at[c, u], "pix", first[h])

    def relay_copy(c, u, h):
        part = held(c, u).at[part_at(first[h], h)]
        return send_copy(part, part, 0, relay_r.at[c, u], "pix", second[h])

    def a_copy(c, u, e):
        rows = rows_at(SPLIT_SUM, c, u)
        peer = tm_at(e)
        source = x_buf.at[c, peer, rows]
        return send_copy(source, xt_buf.at[c, me_t, rows], 1, a_r.at[c], "tm", peer)

    def b_copy(c, u, e):
        rows = rows_at(SPLIT_TRACE, c, u)
        peer = tm_at(e)
        target = held(c, u).at[me_p * n_tm + me_t]
        return send_copy(y_buf.at[c, peer, rows], target, 1, b_r.at[c, u], "tm", peer)

    def send_far(c, u=0):
        for h in range(HALVES):
            far_copy(c, u, h).start()

    def send_near(c, u=0):
        for h in range(HALVES):
            near_copy(c, u, h).start()

    def send_hop(c, u=0):
        rows = rows_at(SPLIT_SUM, c, u)
        arrived(far_buf.at[c, :, :, rows], far_r.at[c, u])
        for h in range(HALVES):
            for g in range(parts_half):
                own = part_ref[c, second[h] * n_tm + h * parts_half + g, rows]
                total = own.astype(jnp.float32) + far_buf[c, h, g, rows].astype(jnp.float32)
                hop_out[c, h, g, rows] = total.astype(hop_out.dtype)
            hop_copy(c, u, h).start()

    def sum_chunk(c, u=0):
        rows = rows_at(SPLIT_SUM, c, u)
        arrived(in_buf.at[c, :, :, :, rows], in_r.at[c, u])
        for h in range(HALVES):
            for g in range(parts_half):
                part = h * parts_half + g
                total = part_ref[c, me_p * n_tm + part, rows].astype(jnp.float32)
                total = total + in_buf[c, 0, h, g, rows].astype(jnp.float32)
                total = total + in_buf[c, 1, h, g, rows].astype(jnp.float32)
                x_buf[c, part, rows] = total.astype(x_buf.dtype)
        for e in far_first:
            a_copy(c, u, e).start()
        xt_buf[c, me_t, rows] = x_buf[c, me_t, rows]

    def ready_filter():
        load_prec.wait()
        load_band.wait()
        for d in range(prec_ref.shape[0]):
            matrix = prec_ref[d].astype(jnp.float32)
            prec_t[:, d * FR:(d + 1) * FR] = matrix.T.astype(prec_t.dtype)

    def filter_chunk(c):
        groups = LANE // GROUP
        at = ((me_p * n_tm + me_t) * chunks + c) * groups
        column = lax.broadcasted_iota(jnp.int32, (1, LANE), 1)
        reach = jnp.zeros((1, LANE), jnp.int32)
        for g in range(groups):
            reach = jnp.where(column >= g * GROUP, band_ref[at + g], reach)
        keep = [
            jnp.where(reach >= k, 1.0, 0.0).astype(jnp.bfloat16) for k in range(BMAX + 1)
        ]
        arrived(xt_buf.at[c, pl.ds(0, n_tm - 1)], a_r.at[c])

        for i in range(n_tm):
            low, high = max(0, i - BMAX), min(n_tm, i + BMAX + 1)
            source = jnp.concatenate(
                [xt_buf[c, j] * keep[abs(j - i)] for j in range(low, high)], axis=0
            )
            bands = prec_t[:, (low - i + BMAX) * FR:(high - i + BMAX) * FR]
            result = jnp.dot(bands, source, preferred_element_type=jnp.float32)
            y_buf[c, i] = result.T.astype(jnp.bfloat16)

        for u in range(SPLIT_TRACE[c]):
            for e in far_first:
                b_copy(c, u, e).start()
        for u in range(SPLIT_TRACE[c]):
            held(c, u)[me_p * n_tm + me_t] = y_buf[c, me_t, rows_at(SPLIT_TRACE, c, u)]

    def gather_chunk(c, u=0):
        rows = rows_at(SPLIT_TRACE, c, u)
        arrived(y_buf.at[c, pl.ds(0, n_tm - 1), rows], b_r.at[c, u])
        for h in range(HALVES):
            g_copy(c, u, h).start()
        size = FR // SPLIT_TRACE[c]
        span = slice(c * LANE + u * size, c * LANE + (u + 1) * size)
        for j in range(n_tm):
            traces_ref[j, span, :] = held(c, u)[me_p * n_tm + j]

    def relay_chunk(c, u=0):
        arrived(held(c, u).at[pl.ds(0, HALVES * n_tm)], g_r.at[c, u])
        for h in range(HALVES):
            relay_copy(c, u, h).start()

    def each_tile(one_tile):
        def step(k, carry):
            for member in range(batch):
                one_tile(k * batch + member)
            return carry

        lax.fori_loop(0, pieces, step, 0)

    def rebuild_chunk(c):
        for u in range(SPLIT_TRACE[c]):
            arrived(held(c, u).at[pl.ds(0, n_tm)], relay_r.at[c, u])

        def one_tile(n):
            feet = jnp.concatenate([feet_ref[c, n, s] for s in range(slots)], axis=1)
            chosen = jnp.concatenate(
                [
                    held(c, u)[ids_ref[s, n]]
                    for s in range(slots) for u in range(SPLIT_TRACE[c])
                ],
                axis=0,
            )
            rebuilt = jnp.dot(feet, chosen, preferred_element_type=jnp.float32)
            before = base_ref[n] if c > 0 else movie_ref[n].astype(jnp.float32)
            base_ref[n] = before - rebuilt

        each_tile(one_tile)

    half = LANE // 2

    def split_feet():
        def one_tile(n):
            for u, target in ((0, early_ref), (1, half_ref)):
                span = slice(u * half, (u + 1) * half)
                target[n] = jnp.concatenate(
                    [feet_ref[chunks - 1, n, s][:, span] for s in range(slots)], axis=1
                )

        each_tile(one_tile)

    def choose(n, u):
        return jnp.concatenate(
            [held(chunks - 1, u)[ids_ref[s, n]] for s in range(slots)], axis=0
        )

    def rebuild_early():
        arrived(held(chunks - 1, 0).at[pl.ds(0, n_tm)], relay_r.at[chunks - 1, 0])

        def one_tile(n):
            rebuilt = jnp.dot(early_ref[n], choose(n, 0), preferred_element_type=jnp.float32)
            base_ref[n] = base_ref[n] - rebuilt

        each_tile(one_tile)

    def choose_late():
        arrived(held(chunks - 1, 1).at[pl.ds(0, n_tm)], relay_r.at[chunks - 1, 1])

        def one_tile(n):
            chosen_ref[n] = choose(n, 1)

        each_tile(one_tile)

    halves = [slice(u * FR // 2, (u + 1) * FR // 2) for u in range(2)]
    project_part(0)
    put_parts(0, across, halves[0])
    pl.semaphore_wait(barrier, len(first) + n_tm - 1)
    send_far(0, 0)
    for peer in first:
        put_parts(0, peer, halves[0])
    send_near(0, 0)
    project_part(1)
    put_parts(0, across, halves[1])
    send_far(0, 1)
    for peer in first:
        put_parts(0, peer, halves[1])
    put_parts(0, me_p)
    load_prec.start()
    load_band.start()
    for c in range(1, chunks):
        for k in range(pieces):
            feet_load(c, k).start()
    project_chunk(1)
    put_rest(1)
    ready_filter()
    send_far(1, 0)
    send_hop(0, 0)
    send_hop(0, 1)
    send_near(0, 1)
    send_near(1, 0)
    send_hop(1, 0)
    sum_chunk(0, 0)
    send_far(1, 1)
    project_chunk(2)
    put_rest(2)
    send_far(2, 0)
    sum_chunk(0, 1)
    send_near(1, 1)
    send_far(2, 1)
    sum_chunk(1, 0)
    send_near(2, 0)
    filter_chunk(0)
    send_hop(1, 1)
    send_hop(2, 0)
    project_chunk(3)
    put_rest(3)
    send_near(2, 1)
    send_far(3, 0)
    sum_chunk(1, 1)
    send_hop(2, 1)
    sum_chunk(2, 0)
    send_near(3, 0)
    split_feet()
    filter_chunk(1)
    send_hop(3, 0)
    gather_chunk(0, 0)
    sum_chunk(2, 1)
    gather_chunk(1, 0)
    sum_chunk(3, 0)
    relay_chunk(0, 0)
    filter_chunk(2)
    relay_chunk(1, 0)
    filter_chunk(3)
    gather_chunk(2, 0)
    gather_chunk(2, 1)
    relay_chunk(2, 0)
    rebuild_chunk(0)
    gather_chunk(3, 0)
    gather_chunk(3, 1)
    relay_chunk(2, 1)
    relay_chunk(3, 0)
    rebuild_chunk(1)
    relay_chunk(3, 1)
    rebuild_chunk(2)
    rebuild_early()
    choose_late()

    arrived(part_ref, send_sem.at[0])
    arrived(part_ref.at[:, pl.ds(0, blocks - 2)], send_sem.at[1])


def finish_kernel(
    traces_ref, base_ref, half_ref, chosen_ref, traces_hbm, residual_hbm, residual_ref, sem
):
    tiles = base_ref.shape[0]
    batch = tile_batch(tiles)
    copies = [pltpu.make_async_copy(traces_ref, traces_hbm, sem.at[0])]
    copies[0].start()
    for k in range(tiles // batch):
        for member in range(batch):
            n = k * batch + member
            rebuilt = jnp.dot(half_ref[n], chosen_ref[n], preferred_element_type=jnp.float32)
            residual_ref[n] = (base_ref[n] - rebuilt).astype(residual_ref.dtype)
        rows = pl.ds(k * batch, batch)
        copies.append(
            pltpu.make_async_copy(residual_ref.at[rows], residual_hbm.at[rows], sem.at[k + 1])
        )
        copies[-1].start()
    for copy in copies:
        copy.wait()


def finish(traces, base, half, chosen):
    hbm = pl.BlockSpec(memory_space=pl.ANY)
    vmem = pl.BlockSpec(memory_space=pltpu.VMEM)
    held = [
        pltpu.with_memory_space_constraint(x, pltpu.VMEM) for x in (traces, base, half, chosen)
    ]
    tiles = base.shape[0]
    return pl.pallas_call(
        finish_kernel,
        out_shape=[
            jax.ShapeDtypeStruct(traces.shape, jnp.bfloat16),
            jax.ShapeDtypeStruct(base.shape, jnp.bfloat16),
        ],
        in_specs=[vmem] * 4,
        out_specs=[hbm, hbm],
        scratch_shapes=[
            pltpu.VMEM(base.shape, jnp.bfloat16),
            pltpu.SemaphoreType.DMA((tiles // tile_batch(tiles) + 1,)),
        ],
        compiler_params=pltpu.CompilerParams(vmem_limit_bytes=FINISH_LIMIT),
        name="finish",
    )(*held)


def middle(movie, noise_weight, footprints, block_ids, band_width, precision_blocks):
    tiles, slots, pixels, width = footprints.shape
    frames = movie.shape[2]
    chunks, blocks, lanes = width // LANE, K // CBLK, LANE
    n_pix, n_tm = lax.axis_size("pix"), lax.axis_size("tm")
    pieces = tiles // tile_batch(tiles)
    dma = pltpu.SemaphoreType.DMA
    bf16, f32 = jnp.bfloat16, jnp.float32
    vmem = pl.BlockSpec(memory_space=pltpu.VMEM)
    part = (frames, lanes)
    operands = (block_ids.T, band_width, noise_weight, precision_blocks, movie, footprints)
    parts = pl.pallas_call(
        functools.partial(middle_kernel, n_pix, n_tm),
        out_shape=[
            pltpu.VMEM((n_tm, CBLK, frames), bf16),
            pltpu.VMEM(movie.shape, f32),
            pltpu.VMEM((tiles, pixels, slots * lanes // 2), bf16),
            pltpu.VMEM((tiles, slots * lanes // 2, frames), bf16),
        ],
        in_specs=[pl.BlockSpec(memory_space=pl.ANY)] * 6,
        out_specs=[vmem] * 4,
        scratch_shapes=[pltpu.VMEM((chunks, HALVES, n_tm // HALVES) + part, bf16)] * 2 + [
            pltpu.VMEM((chunks, 2, HALVES, n_tm // HALVES) + part, bf16),
            pltpu.VMEM((chunks, n_tm) + part, bf16),
            pltpu.VMEM((chunks, n_tm) + part, bf16),
            pltpu.VMEM((chunks, n_tm, lanes, frames), bf16),
            pltpu.VMEM((FR, precision_blocks.shape[0] * FR), bf16),
            pltpu.VMEM((chunks, tiles, slots, pixels, lanes), bf16),
            pltpu.VMEM((tiles, pixels, slots * lanes // 2), bf16),
            pltpu.VMEM((chunks, blocks) + part, bf16),
            pltpu.VMEM((tiles * slots + 1,) + part, f32),
            pltpu.VMEM((tiles, frames, pixels), bf16),
            pltpu.VMEM(movie.shape, bf16),
            pltpu.VMEM(noise_weight.shape, f32),
            pltpu.VMEM(precision_blocks.shape, bf16),
            pltpu.VMEM((16, LANE), jnp.int32),
            pltpu.SMEM((16, LANE), jnp.int32),
            pltpu.SMEM((slots, tiles), jnp.int32),
            pltpu.SMEM(band_width.shape, jnp.int32),
        ] + [dma((chunks, 2))] * 4 + [dma((chunks,)), dma((chunks, 2)), dma((2,))]
        + [dma((chunks - 1,)), dma((pieces,)), dma((pieces,)), dma((5,))]
        + [pltpu.VMEM((blocks, lanes // n, frames), bf16) for n in SPLIT_TRACE for _ in range(n)],
        compiler_params=pltpu.CompilerParams(
            collective_id=0, has_side_effects=True, vmem_limit_bytes=MIDDLE_LIMIT
        ),
        name="middle",
    )(*[pltpu.with_memory_space_constraint(x, pltpu.HBM) for x in operands])
    traces, residual = finish(*parts)
    return traces.reshape(K // n_pix, frames), residual


def middle_plain(partial_value, movie, footprints, block_ids, band_width, precision_blocks):
    frames = movie.shape[2]
    n_pix, n_tm = lax.axis_size("pix"), lax.axis_size("tm")
    summed = lax.psum_scatter(partial_value, "pix", scatter_dimension=1, tiled=True)
    rows = summed.transpose(1, 0, 3, 2).reshape(K // n_pix, frames)
    moved = lax.all_to_all(rows, "tm", split_axis=0, concat_axis=1, tiled=True)
    here = moved.shape[0]
    start = (lax.axis_index("pix") * n_tm + lax.axis_index("tm")) * here
    widths = lax.dynamic_slice_in_dim(jnp.repeat(band_width, GROUP), start, here)
    nblocks = moved.shape[1] // FR
    padded = jnp.pad(moved.reshape(here, nblocks, FR), ((0, 0), (BMAX, BMAX), (0, 0)))
    filtered = jnp.zeros((here, nblocks, FR), jnp.float32)
    for d in range(2 * BMAX + 1):
        term = jnp.einsum(
            "kbf,fh->kbh", padded[:, d:d + nblocks], precision_blocks[d],
            preferred_element_type=jnp.float32,
        )
        filtered = filtered + jnp.where((abs(d - BMAX) <= widths)[:, None, None], term, 0.0)
    local = filtered.reshape(here, nblocks * FR).astype(jnp.bfloat16)
    traces = lax.all_to_all(local, "tm", split_axis=1, concat_axis=0, tiled=True)
    gathered = lax.all_gather(traces, "pix", axis=0, tiled=True)
    return rebuild(movie, footprints, block_ids, gathered)


def shards(movie, noise_weight, footprints, block_ids, band_width, precision_blocks):
    n_pix, n_tm = lax.axis_size("pix"), lax.axis_size("tm")
    tiles, slots, pixels, width = footprints.shape
    fits = movie.shape[2] == FR and n_pix == SIDE * SIDE and n_pix * n_tm == K // CBLK
    fits = fits and pixels == LANE and tiles * slots <= LANE and width == 4 * LANE
    rest = (movie, footprints, block_ids, band_width, precision_blocks)
    if fits:
        return middle(movie, noise_weight, *rest[1:])
    return middle_plain(project(movie, noise_weight, footprints, block_ids), *rest)


def solution(mesh):
    return jax.shard_map(
        shards,
        mesh=mesh,
        in_specs=(
            P("pix", None, "tm"),
            P("pix", None),
            P("pix", None, None, None),
            P("pix", None),
            P(),
            P(),
        ),
        out_specs=(P("pix", "tm"), P("pix", None, "tm")),
        check_vma=False,
    )
```

```python
import functools

import jax
import jax.numpy as jnp
from jax import lax
from jax.experimental import pallas as pl
from jax.experimental.pallas import tpu as pltpu
from jax.sharding import PartitionSpec as P

K = 16384
CBLK = 512
GROUP = 16
BMAX = 5
FR = 128
LANE = 128
SIDE = 2
HALVES = 2
SPLIT_SUM = (2, 2, 2, 1)
SPLIT_TRACE = (1, 1, 2, 2)
MESH = pl.DeviceIdType.MESH
VMEM_LIMIT = 56 * 1024 * 1024
MIDDLE_LIMIT = 42 * 1024 * 1024
FINISH_LIMIT = 8 * 1024 * 1024


def tile_batch(tiles):
    return 4 if tiles % 4 == 0 else 1


def project_kernel(ids_ref, movie_ref, noise_ref, feet_ref, out_ref, acc_ref):
    tile = pl.program_id(0)

    @pl.when(tile == 0)
    def _():
        acc_ref[...] = jnp.zeros_like(acc_ref)

    batch, slots = feet_ref.shape[:2]
    for member in range(batch):
        at = tile * batch + member
        pixels = movie_ref[member].astype(jnp.float32)
        weighted = (pixels.T * noise_ref[pl.ds(at, 1), :]).astype(jnp.bfloat16)
        products = [
            jnp.dot(weighted, feet_ref[member, slot], preferred_element_type=jnp.float32)
            for slot in range(slots)
        ]
        for slot in range(slots):
            acc_ref[ids_ref[at, slot]] += products[slot]

    @pl.when(tile == pl.num_programs(0) - 1)
    def _():
        def put(b, carry):
            for c in range(out_ref.shape[0]):
                span = slice(c * LANE, (c + 1) * LANE)
                out_ref[c, b] = acc_ref[b, :, span].astype(out_ref.dtype)
            return carry

        lax.fori_loop(0, out_ref.shape[1], put, 0)


def project(movie, noise_weight, footprints, block_ids):
    tiles, slots, pixels, width = footprints.shape
    frames = movie.shape[2]
    blocks = K // CBLK
    batch = tile_batch(tiles)
    shape = (width // LANE, blocks, frames, LANE)
    return pl.pallas_call(
        project_kernel,
        grid_spec=pltpu.PrefetchScalarGridSpec(
            num_scalar_prefetch=1,
            grid=(tiles // batch,),
            in_specs=[
                pl.BlockSpec((batch, pixels, frames), lambda n, ids: (n, 0, 0)),
                pl.BlockSpec((tiles, pixels), lambda n, ids: (0, 0)),
                pl.BlockSpec((batch, slots, pixels, width), lambda n, ids: (n, 0, 0, 0)),
            ],
            out_specs=pl.BlockSpec(shape, lambda n, ids: (0, 0, 0, 0)),
            scratch_shapes=[pltpu.VMEM((blocks, frames, width), jnp.float32)],
        ),
        out_shape=jax.ShapeDtypeStruct(shape, jnp.bfloat16),
        compiler_params=pltpu.CompilerParams(vmem_limit_bytes=VMEM_LIMIT),
        name="project",
    )(block_ids, movie, noise_weight, footprints)


def rebuild_kernel(ids_ref, me_ref, movie_ref, feet_ref, traces_ref, own_ref, out_ref):
    tile = pl.program_id(0)

    @pl.when(tile == 0)
    def _():
        count = own_ref.shape[0]

        def put(b, carry):
            own_ref[b] = traces_ref[me_ref[0] * count + b]
            return carry

        lax.fori_loop(0, count, put, 0)

    batch, slots = feet_ref.shape[:2]
    for member in range(batch):
        at = tile * batch + member
        rebuilt = None
        for slot in range(slots):
            term = jnp.dot(
                feet_ref[member, slot], traces_ref[ids_ref[at, slot]],
                preferred_element_type=jnp.float32,
            )
            rebuilt = term if rebuilt is None else rebuilt + term
        out_ref[member] = (movie_ref[member].astype(jnp.float32) - rebuilt).astype(out_ref.dtype)


def rebuild(movie, footprints, block_ids, traces):
    tiles, slots, pixels, width = footprints.shape
    frames = movie.shape[2]
    blocks = K // CBLK
    n_pix = lax.axis_size("pix")
    batch = tile_batch(tiles)
    own = (blocks // n_pix, width, frames)
    own_traces, residual = pl.pallas_call(
        rebuild_kernel,
        grid_spec=pltpu.PrefetchScalarGridSpec(
            num_scalar_prefetch=2,
            grid=(tiles // batch,),
            in_specs=[
                pl.BlockSpec((batch, pixels, frames), lambda n, ids, me: (n, 0, 0)),
                pl.BlockSpec((batch, slots, pixels, width), lambda n, ids, me: (n, 0, 0, 0)),
                pl.BlockSpec((blocks, width, frames), lambda n, ids, me: (0, 0, 0)),
            ],
            out_specs=[
                pl.BlockSpec(own, lambda n, ids, me: (0, 0, 0)),
                pl.BlockSpec((batch, pixels, frames), lambda n, ids, me: (n, 0, 0)),
            ],
        ),
        out_shape=[
            jax.ShapeDtypeStruct(own, jnp.bfloat16),
            jax.ShapeDtypeStruct(movie.shape, jnp.bfloat16),
        ],
        compiler_params=pltpu.CompilerParams(vmem_limit_bytes=VMEM_LIMIT),
        name="rebuild",
    )(
        block_ids, lax.axis_index("pix").reshape(1),
        movie, footprints, traces.reshape(blocks, width, frames),
    )
    return own_traces.reshape(K // n_pix, frames), residual


def middle_kernel(
    n_pix, n_tm, ids_hbm, band_hbm, noise_hbm, prec_hbm, movie_hbm, feet_hbm,
    traces_ref, base_ref, half_ref, chosen_ref,
    far_buf, hop_out, in_buf, x_buf, xt_buf, y_buf,
    prec_t, feet_ref, early_ref, part_ref, sums_ref, weighted_ref,
    movie_ref, noise_ref, prec_ref, table_ref, table_smem, ids_ref, band_ref,
    far_r, in_r, g_r, b_r, a_r, relay_r, send_sem,
    feet_sem, piece_sem, movie_sem, small_sem, *gathered,
):
    chunks, tiles, slots = feet_ref.shape[:3]
    blocks = part_ref.shape[1]
    parts_half = n_tm // HALVES
    batch = tile_batch(tiles)
    pieces = tiles // batch
    nothing = tiles * slots
    me_p = lax.axis_index("pix")
    me_t = lax.axis_index("tm")
    me_x = lax.rem(me_p, SIDE)
    along_x = me_p + 1 - 2 * me_x
    along_y = lax.rem(me_p + SIDE, n_pix)
    across = lax.rem(along_x + SIDE, n_pix)
    first = (along_x, along_y)
    second = (along_y, along_x)

    far_first = sorted(range(1, n_tm), key=lambda e: abs(2 * e - n_tm))

    def tm_at(e):
        return lax.rem(me_t + e, n_tm)

    def part_at(owner, h):
        return pl.ds(owner * n_tm + h * parts_half, parts_half)

    barrier = pltpu.get_barrier_semaphore()
    for peer in first:
        pl.semaphore_signal(barrier, inc=1, device_id={"pix": peer}, device_id_type=MESH)
    for e in range(1, n_tm):
        pl.semaphore_signal(
            barrier, inc=1, device_id={"tm": tm_at(e)}, device_id_type=MESH
        )

    def feet_load(c, k):
        rows = pl.ds(k * batch, batch)
        return pltpu.make_async_copy(
            feet_hbm.at[rows, :, :, pl.ds(c * LANE, LANE)], feet_ref.at[c, rows],
            piece_sem.at[k] if c == 0 else feet_sem.at[c - 1],
        )

    def movie_load(k):
        rows = pl.ds(k * batch, batch)
        return pltpu.make_async_copy(movie_hbm.at[rows], movie_ref.at[rows], movie_sem.at[k])

    def arrived(ref, sem):
        pltpu.make_async_copy(ref, ref, sem).wait()

    load_ids = pltpu.make_async_copy(ids_hbm, ids_ref, small_sem.at[0])
    load_noise = pltpu.make_async_copy(noise_hbm, noise_ref, small_sem.at[1])
    load_prec = pltpu.make_async_copy(prec_hbm, prec_ref, small_sem.at[2])
    load_band = pltpu.make_async_copy(band_hbm, band_ref, small_sem.at[3])
    move_table = pltpu.make_async_copy(table_ref, table_smem, small_sem.at[4])

    load_ids.start()
    load_noise.start()
    for k in range(pieces):
        movie_load(k).start()
        feet_load(0, k).start()
    sums_ref[nothing] = jnp.zeros(sums_ref.shape[1:], sums_ref.dtype)
    load_ids.wait()

    lane = lax.broadcasted_iota(jnp.int32, (8, LANE), 1)

    named = jnp.zeros((8, LANE), jnp.int32)
    for k in range(nothing):
        named = jnp.where(lane == k, ids_ref[k % slots, k // slots], named)
    prev = jnp.full((8, LANE), nothing, jnp.int32)
    last = prev
    for k in range(nothing):
        block = ids_ref[k % slots, k // slots]
        last = jnp.where(lane == block, k, last)
        prev = jnp.where((named == block) & (lane > k), k, prev)
    table_ref[0:8, :] = prev
    table_ref[8:16, :] = last
    move_table.start()
    load_noise.wait()
    for k in range(pieces):
        movie_load(k).wait()
        for member in range(batch):
            n = k * batch + member
            pixels = movie_ref[n].astype(jnp.float32).T
            weighted_ref[n] = (pixels * noise_ref[n:n + 1, :]).astype(jnp.bfloat16)
    move_table.wait()

    def one_tile(n, c, rows):
        feet = jnp.concatenate([feet_ref[c, n, s] for s in range(slots)], axis=1)
        products = jnp.dot(weighted_ref[n, rows], feet, preferred_element_type=jnp.float32)
        before = [sums_ref[table_smem[0, n * slots + s], rows] for s in range(slots)]
        for s in range(slots):
            total = before[s] + products[:, s * LANE:(s + 1) * LANE]
            sums_ref[n * slots + s, rows] = total

    def project_chunk(c):
        arrived(feet_ref.at[c], feet_sem.at[c - 1])

        def step(k, carry):
            for member in range(batch):
                one_tile(k * batch + member, c, slice(0, FR))
            return carry

        lax.fori_loop(0, pieces, step, 0)

    def project_part(u):
        size = FR // SPLIT_SUM[0]
        for n in range(tiles):
            if u == 0 and n % batch == 0:
                feet_load(0, n // batch).wait()
            one_tile(n, 0, slice(u * size, (u + 1) * size))

    def put_parts(c, owner, rows=slice(0, FR)):
        for j in range(n_tm):
            b = owner * n_tm + j
            part_ref[c, b, rows] = sums_ref[table_smem[8, b], rows].astype(part_ref.dtype)

    def put_rest(c):
        for owner in (across,) + first + (me_p,):
            put_parts(c, owner)

    def unit(split, c, u):
        return sum(split[:c]) + u

    def held(c, u):
        return gathered[unit(SPLIT_TRACE, c, u)]

    def rows_at(split, c, u):
        size = FR // split[c]
        return pl.ds(u * size, size)

    def send_copy(source, target, sends, recv, axis, peer):
        return pltpu.make_async_remote_copy(
            src_ref=source, dst_ref=target, send_sem=send_sem.at[sends], recv_sem=recv,
            device_id={axis: peer}, device_id_type=MESH,
        )

    def far_copy(c, u, h):
        rows = rows_at(SPLIT_SUM, c, u)
        source = part_ref.at[c, part_at(across, h), rows]
        return send_copy(source, far_buf.at[c, h, :, rows], 0, far_r.at[unit(SPLIT_SUM, c, u)], "pix", first[h])

    def near_copy(c, u, h):
        rows = rows_at(SPLIT_SUM, c, u)
        source = part_ref.at[c, part_at(first[h], h), rows]
        return send_copy(source, in_buf.at[c, 0, h, :, rows], 0, in_r.at[unit(SPLIT_SUM, c, u)], "pix", first[h])

    def hop_copy(c, u, h):
        rows = rows_at(SPLIT_SUM, c, u)
        source = hop_out.at[c, h, :, rows]
        return send_copy(source, in_buf.at[c, 1, h, :, rows], 0, in_r.at[unit(SPLIT_SUM, c, u)], "pix", second[h])

    def g_copy(c, u, h):
        part = held(c, u).at[pl.ds(me_p * n_tm, n_tm)]
        return send_copy(part, part, 1, g_r.at[unit(SPLIT_TRACE, c, u)], "pix", first[h])

    def relay_copy(c, u, h):
        part = held(c, u).at[part_at(first[h], h)]
        return send_copy(part, part, 0, relay_r.at[unit(SPLIT_TRACE, c, u)], "pix", second[h])

    def a_copy(c, u, e):
        rows = rows_at(SPLIT_SUM, c, u)
        peer = tm_at(e)
        source = x_buf.at[c, peer, rows]
        return send_copy(source, xt_buf.at[c, me_t, rows], 1, a_r.at[c], "tm", peer)

    def b_copy(c, u, e):
        rows = rows_at(SPLIT_TRACE, c, u)
        peer = tm_at(e)
        target = held(c, u).at[me_p * n_tm + me_t]
        return send_copy(y_buf.at[c, peer, rows], target, 1, b_r.at[unit(SPLIT_TRACE, c, u)], "tm", peer)

    def send_far(c, u=0):
        for h in range(HALVES):
            far_copy(c, u, h).start()

    def send_near(c, u=0):
        for h in range(HALVES):
            near_copy(c, u, h).start()

    def send_hop(c, u=0):
        rows = rows_at(SPLIT_SUM, c, u)
        arrived(far_buf.at[c, :, :, rows], far_r.at[unit(SPLIT_SUM, c, u)])
        for h in range(HALVES):
            for g in range(parts_half):
                own = part_ref[c, second[h] * n_tm + h * parts_half + g, rows]
                total = own.astype(jnp.float32) + far_buf[c, h, g, rows].astype(jnp.float32)
                hop_out[c, h, g, rows] = total.astype(hop_out.dtype)
            hop_copy(c, u, h).start()

    def sum_chunk(c, u=0):
        rows = rows_at(SPLIT_SUM, c, u)
        arrived(in_buf.at[c, :, :, :, rows], in_r.at[unit(SPLIT_SUM, c, u)])
        for h in range(HALVES):
            for g in range(parts_half):
                part = h * parts_half + g
                total = part_ref[c, me_p * n_tm + part, rows].astype(jnp.float32)
                total = total + in_buf[c, 0, h, g, rows].astype(jnp.float32)
                total = total + in_buf[c, 1, h, g, rows].astype(jnp.float32)
                x_buf[c, part, rows] = total.astype(x_buf.dtype)
        for e in far_first:
            a_copy(c, u, e).start()
        xt_buf[c, me_t, rows] = x_buf[c, me_t, rows]

    def ready_filter():
        load_prec.wait()
        load_band.wait()
        for d in range(prec_ref.shape[0]):
            matrix = prec_ref[d].astype(jnp.float32)
            prec_t[:, d * FR:(d + 1) * FR] = matrix.T.astype(prec_t.dtype)

    def filter_chunk(c):
        groups = LANE // GROUP
        at = ((me_p * n_tm + me_t) * chunks + c) * groups
        column = lax.broadcasted_iota(jnp.int32, (1, LANE), 1)
        reach = jnp.zeros((1, LANE), jnp.int32)
        for g in range(groups):
            reach = jnp.where(column >= g * GROUP, band_ref[at + g], reach)
        keep = [
            jnp.where(reach >= k, 1.0, 0.0).astype(jnp.bfloat16) for k in range(BMAX + 1)
        ]
        arrived(xt_buf.at[c, pl.ds(0, n_tm - 1)], a_r.at[c])

        for i in range(n_tm):
            low, high = max(0, i - BMAX), min(n_tm, i + BMAX + 1)
            source = jnp.concatenate(
                [xt_buf[c, j] * keep[abs(j - i)] for j in range(low, high)], axis=0
            )
            bands = prec_t[:, (low - i + BMAX) * FR:(high - i + BMAX) * FR]
            result = jnp.dot(bands, source, preferred_element_type=jnp.float32)
            y_buf[c, i] = result.T.astype(jnp.bfloat16)

        for u in range(SPLIT_TRACE[c]):
            for e in far_first:
                b_copy(c, u, e).start()
        for u in range(SPLIT_TRACE[c]):
            held(c, u)[me_p * n_tm + me_t] = y_buf[c, me_t, rows_at(SPLIT_TRACE, c, u)]

    def gather_chunk(c, u=0):
        rows = rows_at(SPLIT_TRACE, c, u)
        arrived(y_buf.at[c, pl.ds(0, n_tm - 1), rows], b_r.at[unit(SPLIT_TRACE, c, u)])
        for h in range(HALVES):
            g_copy(c, u, h).start()
        size = FR // SPLIT_TRACE[c]
        span = slice(c * LANE + u * size, c * LANE + (u + 1) * size)
        for j in range(n_tm):
            traces_ref[j, span, :] = held(c, u)[me_p * n_tm + j]

    def relay_chunk(c, u=0):
        arrived(held(c, u).at[pl.ds(0, HALVES * n_tm)], g_r.at[unit(SPLIT_TRACE, c, u)])
        for h in range(HALVES):
            relay_copy(c, u, h).start()

    def each_tile(one_tile):
        def step(k, carry):
            for member in range(batch):
                one_tile(k * batch + member)
            return carry

        lax.fori_loop(0, pieces, step, 0)

    def rebuild_chunk(c):
        for u in range(SPLIT_TRACE[c]):
            arrived(held(c, u).at[pl.ds(0, n_tm)], relay_r.at[unit(SPLIT_TRACE, c, u)])

        def one_tile(n):
            feet = jnp.concatenate([feet_ref[c, n, s] for s in range(slots)], axis=1)
            chosen = jnp.concatenate(
                [
                    held(c, u)[ids_ref[s, n]]
                    for s in range(slots) for u in range(SPLIT_TRACE[c])
                ],
                axis=0,
            )
            rebuilt = jnp.dot(feet, chosen, preferred_element_type=jnp.float32)
            before = base_ref[n] if c > 0 else movie_ref[n].astype(jnp.float32)
            base_ref[n] = before - rebuilt

        each_tile(one_tile)

    half = LANE // 2

    def split_feet():
        def one_tile(n):
            for u, target in ((0, early_ref), (1, half_ref)):
                span = slice(u * half, (u + 1) * half)
                target[n] = jnp.concatenate(
                    [feet_ref[chunks - 1, n, s][:, span] for s in range(slots)], axis=1
                )

        each_tile(one_tile)

    def choose(n, u):
        return jnp.concatenate(
            [held(chunks - 1, u)[ids_ref[s, n]] for s in range(slots)], axis=0
        )

    def rebuild_early():
        arrived(held(chunks - 1, 0).at[pl.ds(0, n_tm)], relay_r.at[unit(SPLIT_TRACE, chunks - 1, 0)])

        def one_tile(n):
            rebuilt = jnp.dot(early_ref[n], choose(n, 0), preferred_element_type=jnp.float32)
            base_ref[n] = base_ref[n] - rebuilt

        each_tile(one_tile)

    def choose_late():
        arrived(held(chunks - 1, 1).at[pl.ds(0, n_tm)], relay_r.at[unit(SPLIT_TRACE, chunks - 1, 1)])

        for n in range(tiles):
            chosen_ref[n] = choose(n, 1)

    halves = [slice(u * FR // 2, (u + 1) * FR // 2) for u in range(2)]
    project_part(0)
    put_parts(0, across, halves[0])
    pl.semaphore_wait(barrier, len(first) + n_tm - 1)
    send_far(0, 0)
    for peer in first:
        put_parts(0, peer, halves[0])
    send_near(0, 0)
    project_part(1)
    put_parts(0, across, halves[1])
    send_far(0, 1)
    for peer in first:
        put_parts(0, peer, halves[1])
    put_parts(0, me_p)
    load_prec.start()
    load_band.start()
    for c in range(1, chunks):
        for k in range(pieces):
            feet_load(c, k).start()
    project_chunk(1)
    put_rest(1)
    ready_filter()
    send_far(1, 0)
    send_hop(0, 0)
    send_hop(0, 1)
    send_near(0, 1)
    send_near(1, 0)
    send_hop(1, 0)
    sum_chunk(0, 0)
    send_far(1, 1)
    project_chunk(2)
    put_rest(2)
    send_far(2, 0)
    sum_chunk(0, 1)
    send_near(1, 1)
    send_far(2, 1)
    sum_chunk(1, 0)
    send_near(2, 0)
    filter_chunk(0)
    send_hop(1, 1)
    send_hop(2, 0)
    project_chunk(3)
    put_rest(3)
    send_near(2, 1)
    send_far(3, 0)
    sum_chunk(1, 1)
    send_hop(2, 1)
    sum_chunk(2, 0)
    send_near(3, 0)
    split_feet()
    filter_chunk(1)
    send_hop(3, 0)
    gather_chunk(0, 0)
    sum_chunk(2, 1)
    gather_chunk(1, 0)
    sum_chunk(3, 0)
    relay_chunk(0, 0)
    filter_chunk(2)
    relay_chunk(1, 0)
    filter_chunk(3)
    gather_chunk(2, 0)
    gather_chunk(2, 1)
    relay_chunk(2, 0)
    rebuild_chunk(0)
    gather_chunk(3, 0)
    gather_chunk(3, 1)
    relay_chunk(2, 1)
    relay_chunk(3, 0)
    rebuild_chunk(1)
    relay_chunk(3, 1)
    rebuild_chunk(2)
    rebuild_early()
    choose_late()

    arrived(part_ref, send_sem.at[0])
    arrived(part_ref.at[:, pl.ds(0, blocks - 2)], send_sem.at[1])


def finish_kernel(
    traces_ref, base_ref, half_ref, chosen_ref, traces_hbm, residual_hbm, residual_ref, sem
):
    tiles = base_ref.shape[0]
    batch = tile_batch(tiles)
    copies = [pltpu.make_async_copy(traces_ref, traces_hbm, sem.at[0])]
    copies[0].start()
    for k in range(tiles // batch):
        for member in range(batch):
            n = k * batch + member
            rebuilt = jnp.dot(half_ref[n], chosen_ref[n], preferred_element_type=jnp.float32)
            residual_ref[n] = (base_ref[n] - rebuilt).astype(residual_ref.dtype)
        rows = pl.ds(k * batch, batch)
        copies.append(
            pltpu.make_async_copy(residual_ref.at[rows], residual_hbm.at[rows], sem.at[k + 1])
        )
        copies[-1].start()
    for copy in copies:
        copy.wait()


def finish(traces, base, half, chosen):
    hbm = pl.BlockSpec(memory_space=pl.ANY)
    vmem = pl.BlockSpec(memory_space=pltpu.VMEM)
    held = [
        pltpu.with_memory_space_constraint(x, pltpu.VMEM) for x in (traces, base, half, chosen)
    ]
    tiles = base.shape[0]
    return pl.pallas_call(
        finish_kernel,
        out_shape=[
            jax.ShapeDtypeStruct(traces.shape, jnp.bfloat16),
            jax.ShapeDtypeStruct(base.shape, jnp.bfloat16),
        ],
        in_specs=[vmem] * 4,
        out_specs=[hbm, hbm],
        scratch_shapes=[
            pltpu.VMEM(base.shape, jnp.bfloat16),
            pltpu.SemaphoreType.DMA((tiles // tile_batch(tiles) + 1,)),
        ],
        compiler_params=pltpu.CompilerParams(vmem_limit_bytes=FINISH_LIMIT),
        name="finish",
    )(*held)


def middle(movie, noise_weight, footprints, block_ids, band_width, precision_blocks):
    tiles, slots, pixels, width = footprints.shape
    frames = movie.shape[2]
    chunks, blocks, lanes = width // LANE, K // CBLK, LANE
    n_pix, n_tm = lax.axis_size("pix"), lax.axis_size("tm")
    pieces = tiles // tile_batch(tiles)
    dma = pltpu.SemaphoreType.DMA
    bf16, f32 = jnp.bfloat16, jnp.float32
    vmem = pl.BlockSpec(memory_space=pltpu.VMEM)
    part = (frames, lanes)
    operands = (block_ids.T, band_width, noise_weight, precision_blocks, movie, footprints)
    parts = pl.pallas_call(
        functools.partial(middle_kernel, n_pix, n_tm),
        out_shape=[
            pltpu.VMEM((n_tm, CBLK, frames), bf16),
            pltpu.VMEM(movie.shape, f32),
            pltpu.VMEM((tiles, pixels, slots * lanes // 2), bf16),
            pltpu.VMEM((tiles, slots * lanes // 2, frames), bf16),
        ],
        in_specs=[pl.BlockSpec(memory_space=pl.ANY)] * 6,
        out_specs=[vmem] * 4,
        scratch_shapes=[pltpu.VMEM((chunks, HALVES, n_tm // HALVES) + part, bf16)] * 2 + [
            pltpu.VMEM((chunks, 2, HALVES, n_tm // HALVES) + part, bf16),
            pltpu.VMEM((chunks, n_tm) + part, bf16),
            pltpu.VMEM((chunks, n_tm) + part, bf16),
            pltpu.VMEM((chunks, n_tm, lanes, frames), bf16),
            pltpu.VMEM((FR, precision_blocks.shape[0] * FR), bf16),
            pltpu.VMEM((chunks, tiles, slots, pixels, lanes), bf16),
            pltpu.VMEM((tiles, pixels, slots * lanes // 2), bf16),
            pltpu.VMEM((chunks, blocks) + part, bf16),
            pltpu.VMEM((tiles * slots + 1,) + part, f32),
            pltpu.VMEM((tiles, frames, pixels), bf16),
            pltpu.VMEM(movie.shape, bf16),
            pltpu.VMEM(noise_weight.shape, f32),
            pltpu.VMEM(precision_blocks.shape, bf16),
            pltpu.VMEM((16, LANE), jnp.int32),
            pltpu.SMEM((16, LANE), jnp.int32),
            pltpu.SMEM((slots, tiles), jnp.int32),
            pltpu.SMEM(band_width.shape, jnp.int32),
        ] + [dma((sum(SPLIT_SUM),))] * 2 + [dma((sum(SPLIT_TRACE),))] * 2
        + [dma((chunks,)), dma((sum(SPLIT_TRACE),)), dma((2,))]
        + [dma((chunks - 1,)), dma((pieces,)), dma((pieces,)), dma((5,))]
        + [pltpu.VMEM((blocks, lanes // n, frames), bf16) for n in SPLIT_TRACE for _ in range(n)],
        compiler_params=pltpu.CompilerParams(
            collective_id=0, has_side_effects=True, vmem_limit_bytes=MIDDLE_LIMIT
        ),
        name="middle",
    )(*[pltpu.with_memory_space_constraint(x, pltpu.HBM) for x in operands])
    traces, residual = finish(*parts)
    return traces.reshape(K // n_pix, frames), residual


def middle_plain(partial_value, movie, footprints, block_ids, band_width, precision_blocks):
    frames = movie.shape[2]
    n_pix, n_tm = lax.axis_size("pix"), lax.axis_size("tm")
    summed = lax.psum_scatter(partial_value, "pix", scatter_dimension=1, tiled=True)
    rows = summed.transpose(1, 0, 3, 2).reshape(K // n_pix, frames)
    moved = lax.all_to_all(rows, "tm", split_axis=0, concat_axis=1, tiled=True)
    here = moved.shape[0]
    start = (lax.axis_index("pix") * n_tm + lax.axis_index("tm")) * here
    widths = lax.dynamic_slice_in_dim(jnp.repeat(band_width, GROUP), start, here)
    nblocks = moved.shape[1] // FR
    padded = jnp.pad(moved.reshape(here, nblocks, FR), ((0, 0), (BMAX, BMAX), (0, 0)))
    filtered = jnp.zeros((here, nblocks, FR), jnp.float32)
    for d in range(2 * BMAX + 1):
        term = jnp.einsum(
            "kbf,fh->kbh", padded[:, d:d + nblocks], precision_blocks[d],
            preferred_element_type=jnp.float32,
        )
        filtered = filtered + jnp.where((abs(d - BMAX) <= widths)[:, None, None], term, 0.0)
    local = filtered.reshape(here, nblocks * FR).astype(jnp.bfloat16)
    traces = lax.all_to_all(local, "tm", split_axis=1, concat_axis=0, tiled=True)
    gathered = lax.all_gather(traces, "pix", axis=0, tiled=True)
    return rebuild(movie, footprints, block_ids, gathered)


def shards(movie, noise_weight, footprints, block_ids, band_width, precision_blocks):
    n_pix, n_tm = lax.axis_size("pix"), lax.axis_size("tm")
    tiles, slots, pixels, width = footprints.shape
    fits = movie.shape[2] == FR and n_pix == SIDE * SIDE and n_pix * n_tm == K // CBLK
    fits = fits and pixels == LANE and tiles * slots <= LANE and width == 4 * LANE
    rest = (movie, footprints, block_ids, band_width, precision_blocks)
    if fits:
        return middle(movie, noise_weight, *rest[1:])
    return middle_plain(project(movie, noise_weight, footprints, block_ids), *rest)


def solution(mesh):
    return jax.shard_map(
        shards,
        mesh=mesh,
        in_specs=(
            P("pix", None, "tm"),
            P("pix", None),
            P("pix", None, None, None),
            P("pix", None),
            P(),
            P(),
        ),
        out_specs=(P("pix", "tm"), P("pix", None, "tm")),
        check_vma=False,
    )
```
